32 devices in a mesh: rows: 8 (over z, x), cols: 4 (over y, core).
Axes of the slice: x: 2, y: 2, z: 4, core: 2. Of those that a mesh axis runs over, the one named last changes fastest.
Arguments:
- cell_bin: int32 [1048576], P(('rows', 'cols')), may hold values from 0 to 32767
- cell_area: bfloat16 [1048576], P(('rows', 'cols')), may hold values from 0.5 to 4
- owner: int32 [1048576], P(('rows', 'cols')), may hold values from 0 to 31, as said below
- net_box: int32 [4, 524288], P(None, ('rows', 'cols')), may hold values from 0 to 511, as said below
Outputs:
- density: float32 [512, 2048], P('rows', 'cols')
- migrated: float32 [3, 2097152], P(None, ('rows', 'cols'))
- migrated_bin: int32 [2097152], P(('rows', 'cols'))
The draws below stay inside these ranges and needn't reach their ends.
Inputs may be any that keep to these rules, and one draw needn't show every extreme that they name: No tile names one owner for more than 2048 of its cells, and some owner is named exactly 2048 times by every tile. `net_box`: each column holds a box inside the net's tile with first row <= last row < 64 and first column <= last column.
All inputs are finite; a program needn't handle non-finite values.
Results may differ from the reference program's by a relative error of at most 0.0003.
Values sent between devices are 32-bit elements; how exact they have to be, the bound alone decides.
No kernel may reach another device: no remote copies, remote signals or barrier semaphores. Data moves between devices by JAX's collectives and lax.ppermute only.
A program may use at most 192 MiB of HBM per device.

```python
import math
import jax
import jax.numpy as jnp
from jax import lax

TILE_R = 64
TILE_C = 512
CELLS_DEV = 32768
NETS_DEV = 16384
SPAN = 16
DIFF_STEPS = 4
CAP = 2048
GRID_R = 512
GRID_C = 2048
TOTAL_CELLS = 1048576
N_ROWS = 8
N_COLS = 4


def draw_owner(key, part):
    devices = N_ROWS * N_COLS
    slots = devices * CAP
    key_order, key_busy, key_tiles = jax.random.split(key, 3)
    order = jax.random.permutation(key_order, devices).astype(jnp.int32)
    busiest = jax.random.randint(key_busy, (), 0, devices)
    reach = 1 + 4096 // (1 + order)
    slot_owner = jnp.arange(slots, dtype=jnp.int32) // CAP
    reach_slot = reach[slot_owner]

    def one_tile(sub):
        key_level, key_tie, key_mix = jax.random.split(sub, 3)
        level = jax.random.randint(key_level, (slots,), 0, reach_slot)
        level = jnp.where(slot_owner == busiest, 4097, level)
        score = level * slots + jax.random.permutation(key_tie, slots).astype(jnp.int32)
        unused, picked = lax.top_k(score, CELLS_DEV)
        chosen = (picked // CAP).astype(jnp.int32)
        return chosen[jax.random.permutation(key_mix, CELLS_DEV)]
    keys = jax.random.split(key_tiles, devices)
    return jax.vmap(one_tile)(keys).reshape(-1).astype(jnp.int32)


def draw_net_box(key, part):
    total = NETS_DEV * N_ROWS * N_COLS
    key_tall, key_wide, key_top, key_left = jax.random.split(key, 4)
    tall = jax.random.randint(key_tall, (total,), 1, SPAN + 1)
    wide = jax.random.randint(key_wide, (total,), 1, SPAN + 1)
    top = jax.random.randint(key_top, (total,), 0, TILE_R - tall + 1)
    first_col = jax.random.randint(key_left, (total,), 0, TILE_C - wide + 1)
    leading = jnp.arange(total, dtype=jnp.int32) % NETS_DEV == 0
    top = jnp.where(leading, 0, top)
    first_col = jnp.where(leading, TILE_C - wide, first_col)
    return jnp.stack([top, top + tall - 1, first_col, first_col + wide - 1]).astype(jnp.int32)


def with_ends(result, key, low, largest):
    extent = result.shape
    place = [jax.random.randint(jax.random.fold_in(key, axis), (), 0, extent[axis]) for axis in range(len(extent))]
    result = result.at[tuple(place)].set(low)
    longest = extent.index(max(extent))
    place[longest] = (place[longest] + 1) % extent[longest]
    return result.at[tuple(place)].set(largest)


def block_scale(key, dims, cuts, least, top_value):
    def one(dim, shards_of):
        heights = jax.random.uniform(jax.random.fold_in(jax.random.fold_in(key, 6), dim), (shards_of,), jnp.float32, least / len(cuts), top_value / len(cuts))
        return jnp.repeat(jnp.exp(heights), dims[dim] // shards_of).reshape((-1,) + (1,) * (len(dims) - dim - 1))

    level = one(*cuts[0])
    for cut in cuts[1:]:
        level = level * one(*cut)
    return level


def setup_inputs(seed: int = 0) -> dict:
    splits = jax.random.split(jax.random.key(seed), 5)
    cell_bin = with_ends(jax.random.randint(splits[0], (TOTAL_CELLS,), 0, TILE_R * TILE_C), jax.random.fold_in(splits[0], 1), 0, (TILE_R * TILE_C) - 1).astype(jnp.int32)
    cell_area = jnp.clip(jnp.exp(math.log(4.0) - 2.0794415 * jax.random.uniform(splits[1], (TOTAL_CELLS,), jnp.float32) ** block_scale(splits[1], (TOTAL_CELLS,), ((0, 32),), -0.2, 0.2)), 0.5, 4.0).astype(jnp.bfloat16)
    owner = draw_owner(jax.random.fold_in(splits[4], 71), 0)
    net_box = draw_net_box(jax.random.fold_in(splits[4], 71), 0)
    return dict(cell_bin=cell_bin, cell_area=cell_area, owner=owner, net_box=net_box)


RATE = 0.2
GAMMA = 0.05


def diffuse(dens, open_lower, open_upper, open_right, open_left):
    padded = jnp.pad(dens, 1)
    lower = (padded[2:, 1:-1] - dens) * open_lower
    upper = (padded[:-2, 1:-1] - dens) * open_upper
    right = (padded[1:-1, 2:] - dens) * open_right
    left = (padded[1:-1, :-2] - dens) * open_left
    spread = 2.0 * (dens + 1.0)
    after = dens + RATE * ((lower + upper) + (right + left))
    return after, -(lower - upper) / spread, -(right - left) / spread


def rank_tile(owners):
    devices = N_ROWS * N_COLS
    hits = (owners[:, None] == jnp.arange(devices, dtype=jnp.int32)[None, :]).astype(jnp.int32)
    before = jnp.cumsum(hits, axis=0) - hits
    return jnp.sum(before * hits, axis=1).astype(jnp.int32)


def reference(cell_bin, cell_area, owner, net_box):
    devices = N_ROWS * N_COLS
    cell_tile = jnp.arange(devices * CELLS_DEV, dtype=jnp.int32) // CELLS_DEV
    grid_row = (cell_tile // N_COLS) * TILE_R + cell_bin // TILE_C
    grid_col = (cell_tile % N_COLS) * TILE_C + cell_bin % TILE_C
    area = cell_area.astype(jnp.float32)
    raw = jnp.zeros((GRID_R, GRID_C), jnp.float32).at[grid_row, grid_col].add(area)

    net_tile = jnp.arange(devices * NETS_DEV, dtype=jnp.int32) // NETS_DEV
    row_shift = (net_tile // N_COLS) * TILE_R
    col_shift = (net_tile % N_COLS) * TILE_C
    top = net_box[0] + row_shift
    bottom = net_box[1] + row_shift
    first_col = net_box[2] + col_shift
    last_col = net_box[3] + col_shift
    tall = (net_box[1] - net_box[0] + 1).astype(jnp.float32)
    wide = (net_box[3] - net_box[2] + 1).astype(jnp.float32)
    weight = ((tall + wide) / (tall * wide)).astype(jnp.bfloat16)
    weight = lax.optimization_barrier(weight).astype(jnp.float32)
    marks = jnp.zeros((GRID_R + 1, GRID_C + 1), jnp.float32)
    marks = marks.at[top, first_col].add(weight)
    marks = marks.at[top, last_col + 1].add(-weight)
    marks = marks.at[bottom + 1, first_col].add(-weight)
    marks = marks.at[bottom + 1, last_col + 1].add(weight)
    congestion = jnp.cumsum(jnp.cumsum(marks, axis=0), axis=1)[:GRID_R, :GRID_C]
    dens = raw * (1.0 + GAMMA * congestion)

    row_index = lax.broadcasted_iota(jnp.int32, (GRID_R, 1), 0)
    col_index = lax.broadcasted_iota(jnp.int32, (1, GRID_C), 1)
    open_lower = (row_index + 1 < GRID_R).astype(jnp.float32)
    open_upper = (row_index >= 1).astype(jnp.float32)
    open_right = (col_index + 1 < GRID_C).astype(jnp.float32)
    open_left = (col_index >= 1).astype(jnp.float32)
    flow_row = jnp.zeros((GRID_R, GRID_C), jnp.float32)
    flow_col = jnp.zeros((GRID_R, GRID_C), jnp.float32)
    for step in range(DIFF_STEPS):
        dens, speed_row, speed_col = diffuse(dens, open_lower, open_upper, open_right, open_left)
        flow_row = flow_row + speed_row
        flow_col = flow_col + speed_col

    shift_row = flow_row[grid_row, grid_col]
    shift_col = flow_col[grid_row, grid_col]
    ranks = lax.map(rank_tile, owner.reshape(devices, CELLS_DEV)).reshape(-1)
    records = jnp.stack([shift_row, shift_col, area, cell_bin.astype(jnp.float32)])
    filler = jnp.concatenate([jnp.zeros((3, devices, devices, CAP), jnp.float32),
                              -jnp.ones((1, devices, devices, CAP), jnp.float32)])
    placed = filler.at[:, owner, cell_tile, ranks].set(records)
    migrated = placed[:3].reshape(3, -1)
    migrated_bin = placed[3].reshape(-1).astype(jnp.int32)
    return dens, migrated, migrated_bin
```

```python
import functools
import jax
import jax.numpy as jnp
from jax import lax
from jax.experimental import pallas as pl
from jax.experimental.pallas import tpu as pltpu
from jax.sharding import PartitionSpec as P

TILE_R = 64
TILE_C = 512
DIFF_STEPS = 4
RATE = 0.2
GAMMA = 0.05
LANES = 128
EDGE = 8
GROUP = 16
BF16 = jnp.bfloat16
F32 = jnp.float32


def dot_nt(a, b):
    return lax.dot_general(a, b, (((1,), (1,)), ((), ())), preferred_element_type=F32)


def sublane_iota(rows, lanes=LANES):
    return lax.broadcasted_iota(jnp.int32, (rows, lanes), 0)


def narrow(x):
    return x.astype(F32).astype(BF16)


def spread(row, rows):
    lanes = row.shape[1]
    packed = jnp.broadcast_to(row, (16, lanes)).astype(BF16)
    return jnp.broadcast_to(packed[None], (rows // 16, 16, lanes)).reshape(rows, lanes)


def density_kernel(bin_ref, area_ref, box_ref, dens_ref, top_ref, bottom_ref, s_ref, w_ref, a_ref, raw_ref, cong_ref):
    bins = bin_ref[...]
    s_ref[...] = (((bins >> 8) & 1) * TILE_R + (bins >> 9)).astype(F32)
    w_ref[...] = (bins & 255).astype(F32)
    a_ref[...] = area_ref[...].astype(F32)
    raw_ref[...] = jnp.zeros_like(raw_ref)
    cong_ref[...] = jnp.zeros_like(cong_ref)
    nil = jnp.zeros((), BF16)
    one = jnp.ones((), BF16)
    s_iota = narrow(sublane_iota(2 * TILE_R))
    w_iota = narrow(sublane_iota(256))

    def cells(step, carry):
        left, right = [], []
        for k in range(GROUP):
            r = step * GROUP + k
            here = pl.ds(r, 1)
            hit = s_iota == spread(s_ref[here, :], 2 * TILE_R)
            left.append(jnp.where(hit, spread(a_ref[here, :], 2 * TILE_R), nil))
            right.append(jnp.where(w_iota == spread(w_ref[here, :], 256), one, nil))
        raw_ref[...] += dot_nt(jnp.concatenate(left, axis=1), jnp.concatenate(right, axis=1))
        return carry

    lax.fori_loop(0, bin_ref.shape[0] // GROUP, cells, 0)
    width = GROUP * LANES
    r_iota = narrow(sublane_iota(TILE_R, width))
    c_iota = narrow(sublane_iota(TILE_C, width) - TILE_C // 2)

    def nets(step, carry):
        box = box_ref[:, pl.ds(pl.multiple_of(step * width, width), width)].astype(F32)
        tall = box[1:2] - box[0:1] + 1.0
        wide = box[3:4] - box[2:3] + 1.0
        weight = (tall + wide) / (tall * wide)
        rows = (r_iota >= spread(box[0:1], TILE_R)) & (r_iota <= spread(box[1:2], TILE_R))
        half = float(TILE_C // 2)
        cols = (c_iota >= spread(box[2:3] - half, TILE_C)) & (c_iota <= spread(box[3:4] - half, TILE_C))
        cong_ref[...] += dot_nt(
            jnp.where(rows, one, nil), jnp.where(cols, spread(weight, TILE_C), nil)
        )
        return carry

    lax.fori_loop(0, box_ref.shape[1] // width, nets, 0)
    raw = jnp.concatenate([raw_ref[:TILE_R], raw_ref[TILE_R:]], axis=1)
    dens = raw * (1.0 + GAMMA * cong_ref[...])
    dens_ref[...] = dens
    top_ref[...] = dens[:EDGE]
    bottom_ref[...] = dens[TILE_R - EDGE :]


def expand(parts, starts_ref, total, pairs):
    per = pairs[0][2].shape[-2]
    lane = lax.broadcasted_iota(jnp.int32, (per, LANES), 1)
    place = sublane_iota(per) * LANES + lane

    def one_owner(o, carry):
        start = starts_ref[0, o]
        stop = jnp.where(o + 1 < parts, starts_ref[0, jnp.minimum(o + 1, parts - 1)], total)
        row = start // LANES
        shift = start - row * LANES
        back = lax.rem(LANES - shift, LANES)
        keep = place < stop - start
        near = lane < LANES - shift
        for source, slot, target, fill in pairs:
            a = pltpu.roll(source[pl.ds(row, per), :], back, 1)
            b = pltpu.roll(source[pl.ds(row + 1, per), :], back, 1)
            target[o, slot] = jnp.where(keep, jnp.where(near, a, b), fill)
        return carry

    lax.fori_loop(0, parts, one_owner, 0)


def order_kernel(parts, owner_ref, bin_ref, area_ref, slots_ref, sorted_ref, starts_ref,
                 pre_ref, cnt_ref, s_ref, w_ref, bh_ref, bl_ref, ar_ref, acc_ref, b_ref, a_ref, vec_ref, smem_ref, sem):
    rows = owner_ref.shape[0]
    i = sublane_iota(LANES, 2 * LANES)
    j = lax.broadcasted_iota(jnp.int32, (LANES, 2 * LANES), 1)
    upper = narrow(i < j)
    block = 64
    lane = lax.broadcasted_iota(jnp.int32, (block, LANES), 1)
    many = 8

    def rank_rows(c, carry):
        here = pl.ds(pl.multiple_of(c * block, block), block)
        owner = owner_ref[here, :]

        def step(g, both):
            prefix, counts = both
            hits = [owner == g * many + k for k in range(many)]
            sums = jnp.dot(jnp.concatenate([narrow(h) for h in hits], axis=0), upper, preferred_element_type=F32)
            for k in range(many):
                part = sums[k * block : (k + 1) * block]
                prefix = jnp.where(hits[k], part[:, :LANES], prefix)
                counts = jnp.where(lane == g * many + k, part[:, LANES:], counts)
            return prefix, counts

        zero = jnp.zeros((block, LANES), F32)
        prefix, counts = lax.fori_loop(0, parts // many, step, (zero, zero))
        pre_ref[here, :] = prefix
        cnt_ref[here, :] = counts
        return carry

    lax.fori_loop(0, rows // block, rank_rows, 0)
    counts = cnt_ref[...]
    lower = narrow(lax.broadcasted_iota(jnp.int32, (rows, rows), 1) < lax.broadcasted_iota(jnp.int32, (rows, rows), 0))
    base = jnp.dot(lower, counts.astype(BF16), preferred_element_type=F32)
    total = base[rows - 8 :] + counts[rows - 8 :]
    high = jnp.floor(total * (1.0 / 64.0))
    low = total - high * 64.0
    strict = upper[:, :LANES]
    first = jnp.dot(low.astype(BF16), strict, preferred_element_type=F32) + 64.0 * jnp.dot(
        high.astype(BF16), strict, preferred_element_type=F32
    )
    starts = jnp.broadcast_to(first[7:8], (8, LANES))
    vec_ref[...] = starts.astype(jnp.int32)
    starts_ref[...] = starts.astype(jnp.int32)
    copy = pltpu.make_async_copy(vec_ref, smem_ref, sem)
    copy.start()
    dest = (pre_ref[...] + jnp.take_along_axis(base + starts[:1], owner_ref[...], axis=1)).astype(jnp.int32)
    half = rows // 2
    top = jnp.where(dest >= half * LANES, 1, 0)
    s_ref[...] = ((dest >> 7) - top * half).astype(F32)
    w_ref[...] = ((dest & (LANES - 1)) + top * LANES).astype(F32)
    bins = bin_ref[...]
    bh_ref[...] = (bins >> 8).astype(F32)
    bl_ref[...] = (bins & 255).astype(F32)
    ar_ref[...] = area_ref[...].astype(F32)
    acc_ref[...] = jnp.zeros_like(acc_ref)
    nil = jnp.zeros((), BF16)
    one = jnp.ones((), BF16)
    s_iota = narrow(sublane_iota(half))
    w_iota = narrow(sublane_iota(2 * LANES))

    def place(step, carry):
        left, right = [], []
        for k in range(GROUP):
            here = pl.ds(step * GROUP + k, 1)
            hit = s_iota == spread(s_ref[here, :], half)
            left.append(
                jnp.concatenate(
                    [jnp.where(hit, spread(x[here, :], half), nil) for x in (bh_ref, bl_ref, ar_ref)], axis=0
                )
            )
            right.append(jnp.where(w_iota == spread(w_ref[here, :], 2 * LANES), one, nil))
        acc_ref[...] += dot_nt(jnp.concatenate(left, axis=1), jnp.concatenate(right, axis=1))
        return carry

    lax.fori_loop(0, rows // GROUP, place, 0)
    for h in range(2):
        cols = slice(h * LANES, (h + 1) * LANES)
        out = slice(h * half, (h + 1) * half)
        b_ref[out, :] = acc_ref[:half, cols] * 256.0 + acc_ref[half : 2 * half, cols]
        a_ref[out, :] = acc_ref[2 * half :, cols]
    pad = slice(rows, b_ref.shape[0])
    b_ref[pad, :] = jnp.zeros((b_ref.shape[0] - rows, LANES), F32)
    a_ref[pad, :] = jnp.zeros((b_ref.shape[0] - rows, LANES), F32)
    sorted_ref[...] = b_ref[:rows]
    copy.wait()
    expand(parts, smem_ref, rows * LANES, ((b_ref, 0, slots_ref, -1.0), (a_ref, 1, slots_ref, 0.0)))


def flow_kernel(parts, grid_rows, grid_cols, starts_ref, place_ref, dens_in, up_ref, down_ref, left_ref, right_ref, sorted_ref,
                dens_ref, slots_ref, pad_ref, hi_ref, lo_ref, row_ref, col_ref):
    rows = sorted_ref.shape[0]
    mid = pl.ds(EDGE, TILE_R)
    inner = pl.ds(LANES, TILE_C)
    pad_ref[mid, inner] = dens_in[...]
    pad_ref[:EDGE, inner] = up_ref[...]
    pad_ref[TILE_R + EDGE :, inner] = down_ref[...]
    pad_ref[:, :LANES] = left_ref[...]
    pad_ref[:, LANES + TILE_C :] = right_ref[...]
    tall, wide = pad_ref.shape
    grow = place_ref[0] + lax.broadcasted_iota(jnp.int32, (tall, 1), 0) - EDGE
    gcol = place_ref[1] + lax.broadcasted_iota(jnp.int32, (1, wide), 1) - LANES
    open_lower = grow + 1 != grid_rows
    open_upper = grow != 0
    open_right = gcol + 1 != grid_cols
    open_left = gcol != 0
    flow_row = jnp.zeros((TILE_R, TILE_C), F32)
    flow_col = jnp.zeros((TILE_R, TILE_C), F32)
    for step in range(DIFF_STEPS):
        d = pad_ref[...]
        lower = jnp.where(open_lower, pltpu.roll(d, tall - 1, 0) - d, 0.0)
        upper = jnp.where(open_upper, pltpu.roll(d, 1, 0) - d, 0.0)
        right = jnp.where(open_right, pltpu.roll(d, wide - 1, 1) - d, 0.0)
        left = jnp.where(open_left, pltpu.roll(d, 1, 1) - d, 0.0)
        pad_ref[...] = d + RATE * ((lower + upper) + (right + left))
        centre = (slice(EDGE, EDGE + TILE_R), slice(LANES, LANES + TILE_C))
        rate = -0.5 / (d[centre] + 1.0)
        flow_row += (lower - upper)[centre] * rate
        flow_col += (right - left)[centre] * rate
    dens_ref[...] = pad_ref[mid, inner]
    coarse, fine = [], []
    for flow in (flow_row, flow_col):
        table = jnp.concatenate([flow[:, k * LANES : (k + 1) * LANES] for k in range(TILE_C // LANES)], axis=0).T
        big = table.astype(BF16)
        coarse.append(big)
        fine.append((table - big.astype(F32)).astype(BF16))
    table = jnp.concatenate(coarse + fine, axis=0)
    bins = sorted_ref[...].astype(jnp.int32)
    hi_ref[...] = (((bins >> 7) & 3) * TILE_R + (bins >> 9)).astype(F32)
    lo_ref[...] = (bins & (LANES - 1)).astype(F32)
    hi_iota = narrow(sublane_iota(256))
    lo_iota = sublane_iota(LANES).astype(F32)
    nil = jnp.zeros((), BF16)
    one = jnp.ones((), BF16)
    group = 8

    def look_up(step, carry):
        picks = jnp.concatenate(
            [
                jnp.where(hi_iota == spread(hi_ref[pl.ds(step * group + k, 1), :], 256), one, nil)
                for k in range(group)
            ],
            axis=1,
        )
        found = jnp.dot(table, picks, preferred_element_type=F32)
        for k in range(group):
            here = pl.ds(step * group + k, 1)
            hit = lo_iota == lo_ref[here, :]
            part = found[:, k * LANES : (k + 1) * LANES]
            both = part[: 2 * LANES] + part[2 * LANES :]
            row_ref[here, :] = jnp.sum(jnp.where(hit, both[:LANES], 0.0), axis=0, keepdims=True)
            col_ref[here, :] = jnp.sum(jnp.where(hit, both[LANES:], 0.0), axis=0, keepdims=True)
        return carry

    lax.fori_loop(0, rows // group, look_up, 0)
    pad = slice(rows, row_ref.shape[0])
    row_ref[pad, :] = jnp.zeros((row_ref.shape[0] - rows, LANES), F32)
    col_ref[pad, :] = jnp.zeros((row_ref.shape[0] - rows, LANES), F32)
    expand(parts, starts_ref, rows * LANES, ((row_ref, 0, slots_ref, 0.0), (col_ref, 1, slots_ref, 0.0)))


def shape(*dims, dtype=F32):
    return jax.ShapeDtypeStruct(dims, dtype)


def vmem(*dims, dtype=F32):
    return pltpu.VMEM(dims, dtype)


def on_device(cell_bin, cell_area, owner, net_box):
    parts = lax.axis_size(("rows", "cols"))
    count = cell_bin.shape[0]
    rows = count // LANES
    capacity = 2 * count // parts
    per = capacity // LANES
    spare = -(-(per + 1) // 8) * 8
    bins = cell_bin.reshape(rows, LANES)
    area = cell_area.reshape(rows, LANES)
    n_rows, n_cols = lax.axis_size("rows"), lax.axis_size("cols")
    grid_rows, grid_cols = n_rows * TILE_R, n_cols * TILE_C
    dens, top, bottom = pl.pallas_call(
        density_kernel,
        out_shape=(shape(TILE_R, TILE_C), shape(EDGE, TILE_C), shape(EDGE, TILE_C)),
        scratch_shapes=[vmem(rows, LANES)] * 3 + [vmem(2 * TILE_R, 256), vmem(TILE_R, TILE_C)],
        name="density",
    )(bins, area, net_box)
    ahead = [(k, k + 1) for k in range(n_rows - 1)]
    behind = [(k + 1, k) for k in range(n_rows - 1)]
    up = lax.ppermute(bottom, "rows", ahead)
    down = lax.ppermute(top, "rows", behind)
    slots, in_order, starts = pl.pallas_call(
        functools.partial(order_kernel, parts),
        out_shape=(shape(parts, 2, per, LANES), shape(rows, LANES), shape(8, LANES, dtype=jnp.int32)),
        scratch_shapes=[vmem(rows, LANES)] * 7
        + [vmem(3 * rows // 2, 2 * LANES), vmem(rows + spare, LANES), vmem(rows + spare, LANES),
           vmem(8, LANES, dtype=jnp.int32), pltpu.SMEM((8, LANES), jnp.int32), pltpu.SemaphoreType.DMA],
        cost_estimate=pl.CostEstimate(flops=15_000_000_000, bytes_accessed=2_000_000, transcendentals=0),
        name="order",
    )(owner.reshape(rows, LANES), bins, area)
    strip = jnp.concatenate([up, dens, down], axis=0)
    ahead = [(k, k + 1) for k in range(n_cols - 1)]
    behind = [(k + 1, k) for k in range(n_cols - 1)]
    left = lax.ppermute(strip[:, TILE_C - LANES :], "cols", ahead)
    right = lax.ppermute(strip[:, :LANES], "cols", behind)
    first = lax.all_to_all(slots, ("rows", "cols"), 0, 0, tiled=True)
    place = jnp.stack([lax.axis_index("rows") * TILE_R, lax.axis_index("cols") * TILE_C]).astype(jnp.int32)
    whole = pl.BlockSpec(memory_space=pltpu.VMEM)
    scalars = pl.BlockSpec(memory_space=pltpu.SMEM)
    density, shifts = pl.pallas_call(
        functools.partial(flow_kernel, parts, grid_rows, grid_cols),
        out_shape=(shape(TILE_R, TILE_C), shape(parts, 2, per, LANES)),
        in_specs=[scalars, scalars] + [whole] * 6,
        scratch_shapes=[vmem(TILE_R + 2 * EDGE, TILE_C + 2 * LANES), vmem(rows, LANES), vmem(rows, LANES),
                        vmem(rows + spare, LANES), vmem(rows + spare, LANES)],
        cost_estimate=pl.CostEstimate(flops=15_000_000_000, bytes_accessed=2_000_000, transcendentals=0),
        name="flow",
    )(starts, place, dens, up, down, left, right, in_order)
    second = lax.all_to_all(shifts, ("rows", "cols"), 0, 0, tiled=True)
    migrated = jnp.stack([second[:, 0].reshape(-1), second[:, 1].reshape(-1), first[:, 1].reshape(-1)])
    return density, migrated, first[:, 0].reshape(-1).astype(jnp.int32)


def solution(mesh):
    both = ("rows", "cols")
    in_specs = (P(both), P(both), P(both), P(None, both))
    out_specs = (P("rows", "cols"), P(None, both), P(both))
    return jax.shard_map(on_device, mesh=mesh, in_specs=in_specs, out_specs=out_specs, check_vma=False)
```

```python
import functools
import jax
import jax.numpy as jnp
from jax import lax
from jax.experimental import pallas as pl
from jax.experimental.pallas import tpu as pltpu
from jax.sharding import PartitionSpec as P

TILE_R = 64
TILE_C = 512
DIFF_STEPS = 4
RATE = 0.2
GAMMA = 0.05
LANES = 128
EDGE = 8
GROUP = 32
DIRECT = 8
BY_DOT = 12
BF16 = jnp.bfloat16
F8 = jnp.float8_e4m3fn
SMALL = 64.0
MIDDLE = 16384
F32 = jnp.float32


def dot_nt(a, b):
    return lax.dot_general(a, b, (((1,), (1,)), ((), ())), preferred_element_type=F32)


def sublane_iota(rows, lanes=LANES):
    return lax.broadcasted_iota(jnp.int32, (rows, lanes), 0)


def narrow(x):
    return x.astype(F32).astype(BF16)


def spread(row, rows):
    lanes = row.shape[1]
    packed = jnp.broadcast_to(row, (16, lanes)).astype(BF16)
    return jnp.broadcast_to(packed[None], (rows // 16, 16, lanes)).reshape(rows, lanes)


def halves(x):
    big = x.astype(F8).astype(F32)
    return big, x - big


def density_kernel(bin_ref, area_ref, box_ref, dens_ref, top_ref, bottom_ref, s_ref, w_ref, a_ref, b_ref, raw_ref, cong_ref):
    bins = bin_ref[...]
    s_ref[...] = (((bins >> 8) & 1) * TILE_R + (bins >> 9)).astype(F32)
    w_ref[...] = (bins & 255).astype(F32)
    a_ref[...], b_ref[...] = halves(area_ref[...].astype(F32))
    raw_ref[...] = jnp.zeros_like(raw_ref)
    cong_ref[...] = jnp.zeros_like(cong_ref)
    nil = jnp.zeros((), BF16)
    one = jnp.ones((), BF16)
    s_iota = narrow(sublane_iota(2 * TILE_R))
    w_iota = narrow(sublane_iota(256))
    steps = 8
    group = bin_ref.shape[0] // steps
    width = box_ref.shape[1] // steps
    r_iota = narrow(sublane_iota(TILE_R, width))
    c_iota = narrow(sublane_iota(TILE_C, width) - TILE_C // 2)

    def step(k, carry):
        left, right = [], []
        for j in range(group):
            here = pl.ds(k * group + j, 1)
            hit = s_iota == spread(s_ref[here, :], 2 * TILE_R)
            left.append(
                jnp.concatenate(
                    [jnp.where(hit, spread(x[here, :], 2 * TILE_R), nil).astype(F8) for x in (a_ref, b_ref)], axis=0
                )
            )
            right.append(jnp.where(w_iota == spread(w_ref[here, :], 256), one, nil).astype(F8))
        raw_ref[...] += dot_nt(jnp.concatenate(left, axis=1), jnp.concatenate(right, axis=1))
        box = box_ref[:, pl.ds(pl.multiple_of(k * width, width), width)].astype(F32)
        tall = box[1:2] - box[0:1] + 1.0
        wide = box[3:4] - box[2:3] + 1.0
        weight = ((tall + wide) / (tall * wide)).astype(BF16).astype(F32)
        big, small = halves(weight)
        rows = (r_iota >= spread(box[0:1], TILE_R)) & (r_iota <= spread(box[1:2], TILE_R))
        middle = float(TILE_C // 2)
        cols = (c_iota >= spread(box[2:3] - middle, TILE_C)) & (c_iota <= spread(box[3:4] - middle, TILE_C))
        cong_ref[...] += dot_nt(
            jnp.where(cols, one, nil).astype(F8),
            jnp.concatenate(
                [jnp.where(rows, spread(x, TILE_R), nil).astype(F8) for x in (big, small * SMALL)], axis=0
            ),
        )
        return carry

    lax.fori_loop(0, steps, step, 0)
    raw = raw_ref[: 2 * TILE_R] + raw_ref[2 * TILE_R :]
    raw = jnp.concatenate([raw[:TILE_R], raw[TILE_R:]], axis=1)
    cong = cong_ref[...].T
    cong = cong[:TILE_R] + cong[TILE_R:] * (1.0 / SMALL)
    dens = raw * (1.0 + GAMMA * cong)
    dens_ref[...] = dens
    top_ref[...] = dens[:EDGE]
    bottom_ref[...] = dens[TILE_R - EDGE :]


def expand(parts, starts_ref, total, pairs):
    per = pairs[0][2].shape[-2]
    lane = lax.broadcasted_iota(jnp.int32, (per, LANES), 1)
    place = sublane_iota(per) * LANES + lane

    def one_owner(o, carry):
        start = starts_ref[0, o]
        stop = jnp.where(o + 1 < parts, starts_ref[0, jnp.minimum(o + 1, parts - 1)], total)
        row = start // LANES
        shift = start - row * LANES
        back = lax.rem(LANES - shift, LANES)
        keep = place < stop - start
        near = lane < LANES - shift
        for source, slot, target, fill in pairs:
            a = pltpu.roll(source[pl.ds(row, per), :], back, 1)
            b = pltpu.roll(source[pl.ds(row + 1, per), :], back, 1)
            target[o, slot] = jnp.where(keep, jnp.where(near, a, b), fill)
        return carry

    lax.fori_loop(0, parts, one_owner, 0, unroll=8)


def order_kernel(parts, owner_ref, bin_ref, area_ref, slots_ref, sorted_ref, starts_ref,
                 pre_ref, cnt_ref, s_ref, w_ref, d2_ref, d1_ref, d0_ref, big_ref, small_ref, acc_ref, b_ref, a_ref, vec_ref, smem_ref, sem):
    rows = owner_ref.shape[0]
    i = sublane_iota(LANES, 2 * LANES)
    j = lax.broadcasted_iota(jnp.int32, (LANES, 2 * LANES), 1)
    upper = narrow(i < j)
    block = 64
    lane = lax.broadcasted_iota(jnp.int32, (block, LANES), 1)
    many = 8

    def rank_rows(c, carry):
        here = pl.ds(pl.multiple_of(c * block, block), block)
        owner = owner_ref[here, :]

        def step(g, both):
            prefix, counts = both
            hits = [owner == g * many + k for k in range(many)]
            sums = jnp.dot(jnp.concatenate([narrow(h) for h in hits], axis=0), upper, preferred_element_type=F32)
            for k in range(many):
                part = sums[k * block : (k + 1) * block]
                prefix = jnp.where(hits[k], part[:, :LANES], prefix)
                counts = jnp.where(lane == g * many + k, part[:, LANES:], counts)
            return prefix, counts

        zero = jnp.zeros((block, LANES), F32)
        prefix, counts = lax.fori_loop(0, parts // many, step, (zero, zero))
        pre_ref[here, :] = prefix
        cnt_ref[here, :] = counts
        return carry

    lax.fori_loop(0, rows // block, rank_rows, 0)
    counts = cnt_ref[...]
    lower = narrow(lax.broadcasted_iota(jnp.int32, (rows, rows), 1) < lax.broadcasted_iota(jnp.int32, (rows, rows), 0))
    base = jnp.dot(lower, counts.astype(BF16), preferred_element_type=F32)
    total = base[rows - 8 :] + counts[rows - 8 :]
    high = jnp.floor(total * (1.0 / 64.0))
    low = total - high * 64.0
    strict = upper[:, :LANES]
    first = jnp.dot(low.astype(BF16), strict, preferred_element_type=F32) + 64.0 * jnp.dot(
        high.astype(BF16), strict, preferred_element_type=F32
    )
    starts = jnp.broadcast_to(first[7:8], (8, LANES))
    vec_ref[...] = starts.astype(jnp.int32)
    starts_ref[...] = starts.astype(jnp.int32)
    copy = pltpu.make_async_copy(vec_ref, smem_ref, sem)
    copy.start()
    dest = (pre_ref[...] + jnp.take_along_axis(base + starts[:1], owner_ref[...], axis=1)).astype(jnp.int32)
    half = rows // 2
    top = jnp.where(dest >= half * LANES, 1, 0)
    s_ref[...] = ((dest >> 7) - top * half).astype(F32)
    w_ref[...] = ((dest & (LANES - 1)) + top * LANES).astype(F32)
    bins = bin_ref[...] - MIDDLE
    d0 = ((bins + 16) & 31) - 16
    rest = (bins - d0) >> 5
    d1 = ((rest + 16) & 31) - 16
    d0_ref[...] = d0.astype(F32)
    d1_ref[...] = d1.astype(F32)
    d2_ref[...] = ((rest - d1) >> 5).astype(F32)
    big_ref[...], small_ref[...] = halves(area_ref[...].astype(F32))
    acc_ref[...] = jnp.zeros_like(acc_ref)
    nil = jnp.zeros((), BF16)
    one = jnp.ones((), BF16)
    s_iota = narrow(sublane_iota(half))
    w_iota = narrow(sublane_iota(2 * LANES))

    def place(step, carry):
        left, right = [], []
        for k in range(GROUP):
            here = pl.ds(step * GROUP + k, 1)
            hit = s_iota == spread(s_ref[here, :], half)
            left.append(
                jnp.concatenate(
                    [jnp.where(hit, spread(x[here, :], half), nil).astype(F8) for x in (d2_ref, d1_ref, d0_ref, big_ref, small_ref)], axis=0
                )
            )
            right.append(jnp.where(w_iota == spread(w_ref[here, :], 2 * LANES), one, nil).astype(F8))
        acc_ref[...] += dot_nt(jnp.concatenate(left, axis=1), jnp.concatenate(right, axis=1))
        return carry

    lax.fori_loop(0, rows // GROUP, place, 0)
    for h in range(2):
        cols = slice(h * LANES, (h + 1) * LANES)
        out = slice(h * half, (h + 1) * half)
        part = [acc_ref[k * half : (k + 1) * half, cols] for k in range(5)]
        b_ref[out, :] = (part[0] * 32.0 + part[1]) * 32.0 + part[2] + float(MIDDLE)
        a_ref[out, :] = part[3] + part[4]
    pad = slice(rows, b_ref.shape[0])
    b_ref[pad, :] = jnp.zeros((b_ref.shape[0] - rows, LANES), F32)
    a_ref[pad, :] = jnp.zeros((b_ref.shape[0] - rows, LANES), F32)
    sorted_ref[...] = b_ref[:rows]
    copy.wait()
    expand(parts, smem_ref, rows * LANES, ((b_ref, 0, slots_ref, -1.0), (a_ref, 1, slots_ref, 0.0)))


def flow_kernel(parts, grid_rows, grid_cols, starts_ref, place_ref, dens_in, up_ref, down_ref, left_ref, right_ref, sorted_ref,
                dens_ref, slots_ref, pad_ref, hi_ref, lo_ref, row_ref, col_ref, table_ref):
    rows = sorted_ref.shape[0]
    mid = pl.ds(EDGE, TILE_R)
    inner = pl.ds(LANES, TILE_C)
    pad_ref[mid, inner] = dens_in[...]
    pad_ref[:EDGE, inner] = up_ref[...]
    pad_ref[TILE_R + EDGE :, inner] = down_ref[...]
    pad_ref[:, :LANES] = left_ref[...]
    pad_ref[:, LANES + TILE_C :] = right_ref[...]
    tall, wide = pad_ref.shape
    grow = place_ref[0] + lax.broadcasted_iota(jnp.int32, (tall, 1), 0) - EDGE
    gcol = place_ref[1] + lax.broadcasted_iota(jnp.int32, (1, wide), 1) - LANES
    open_lower = grow + 1 != grid_rows
    open_upper = grow != 0
    open_right = gcol + 1 != grid_cols
    open_left = gcol != 0
    flow_row = jnp.zeros((TILE_R, TILE_C), F32)
    flow_col = jnp.zeros((TILE_R, TILE_C), F32)
    for step in range(DIFF_STEPS):
        d = pad_ref[...]
        lower = jnp.where(open_lower, pltpu.roll(d, tall - 1, 0) - d, 0.0)
        upper = jnp.where(open_upper, pltpu.roll(d, 1, 0) - d, 0.0)
        right = jnp.where(open_right, pltpu.roll(d, wide - 1, 1) - d, 0.0)
        left = jnp.where(open_left, pltpu.roll(d, 1, 1) - d, 0.0)
        pad_ref[...] = d + RATE * ((lower + upper) + (right + left))
        centre = (slice(EDGE, EDGE + TILE_R), slice(LANES, LANES + TILE_C))
        rate = -0.5 / (d[centre] + 1.0)
        flow_row += (lower - upper)[centre] * rate
        flow_col += (right - left)[centre] * rate
    dens_ref[...] = pad_ref[mid, inner]
    coarse, fine = [], []
    for flow in (flow_row, flow_col):
        table = jnp.concatenate([flow[:, k * LANES : (k + 1) * LANES] for k in range(TILE_C // LANES)], axis=0).T
        big = table.astype(BF16)
        coarse.append(big)
        fine.append((table - big.astype(F32)).astype(BF16))
    table = jnp.concatenate(coarse + fine, axis=0)
    bins = sorted_ref[...].astype(jnp.int32)
    hi_ref[:rows] = (((bins >> 7) & 3) * TILE_R + (bins >> 9)).astype(F32)
    lo_ref[:rows] = (bins & (LANES - 1)).astype(F32)
    hi_ref[rows:] = jnp.zeros((hi_ref.shape[0] - rows, LANES), F32)
    lo_ref[rows:] = jnp.zeros((hi_ref.shape[0] - rows, LANES), F32)
    hi_iota = narrow(sublane_iota(256))
    lo_iota = sublane_iota(LANES).astype(F32)
    nil = jnp.zeros((), BF16)
    one = jnp.ones((), BF16)
    for k in range(TILE_C // LANES):
        cols = slice(k * LANES, (k + 1) * LANES)
        out = slice(k * TILE_R, (k + 1) * TILE_R)
        table_ref[0, out, :] = flow_row[:, cols]
        table_ref[1, out, :] = flow_col[:, cols]

    def look_up(step, carry):
        first = step * (DIRECT + BY_DOT)
        here = pl.ds(first, DIRECT)
        row_here, lane_here = hi_ref[here, :], lo_ref[here, :].astype(jnp.int32)
        got = [jnp.zeros((DIRECT, LANES), F32)] * 2
        for k in range(table_ref.shape[1]):
            hit = row_here == float(k)
            for c in range(2):
                line = jnp.broadcast_to(table_ref[c, k : k + 1, :], (DIRECT, LANES))
                near = jnp.take_along_axis(line, lane_here, axis=1, mode="promise_in_bounds")
                got[c] = jnp.where(hit, near, got[c])
        row_ref[here, :] = got[0]
        col_ref[here, :] = got[1]
        picks = jnp.concatenate(
            [
                jnp.where(hi_iota == spread(hi_ref[pl.ds(first + DIRECT + k, 1), :], 256), one, nil)
                for k in range(BY_DOT)
            ],
            axis=1,
        )
        found = jnp.dot(table, picks, preferred_element_type=F32)
        for k in range(BY_DOT):
            here = pl.ds(first + DIRECT + k, 1)
            hit = lo_iota == lo_ref[here, :]
            part = found[:, k * LANES : (k + 1) * LANES]
            both = part[: 2 * LANES] + part[2 * LANES :]
            row_ref[here, :] = jnp.sum(jnp.where(hit, both[:LANES], 0.0), axis=0, keepdims=True)
            col_ref[here, :] = jnp.sum(jnp.where(hit, both[LANES:], 0.0), axis=0, keepdims=True)
        return carry

    lax.fori_loop(0, -(-rows // (DIRECT + BY_DOT)), look_up, 0)
    pad = slice(rows, row_ref.shape[0])
    row_ref[pad, :] = jnp.zeros((row_ref.shape[0] - rows, LANES), F32)
    col_ref[pad, :] = jnp.zeros((row_ref.shape[0] - rows, LANES), F32)
    expand(parts, starts_ref, rows * LANES, ((row_ref, 0, slots_ref, 0.0), (col_ref, 1, slots_ref, 0.0)))


def shape(*dims, dtype=F32):
    return jax.ShapeDtypeStruct(dims, dtype)


def vmem(*dims, dtype=F32):
    return pltpu.VMEM(dims, dtype)


def on_device(cell_bin, cell_area, owner, net_box):
    parts = lax.axis_size(("rows", "cols"))
    count = cell_bin.shape[0]
    rows = count // LANES
    capacity = 2 * count // parts
    per = capacity // LANES
    spare = -(-max(per + 1, -rows % (DIRECT + BY_DOT)) // 8) * 8
    bins = cell_bin.reshape(rows, LANES)
    area = cell_area.reshape(rows, LANES)
    n_rows, n_cols = lax.axis_size("rows"), lax.axis_size("cols")
    grid_rows, grid_cols = n_rows * TILE_R, n_cols * TILE_C
    dens, top, bottom = pl.pallas_call(
        density_kernel,
        out_shape=(shape(TILE_R, TILE_C), shape(EDGE, TILE_C), shape(EDGE, TILE_C)),
        scratch_shapes=[vmem(rows, LANES)] * 4 + [vmem(4 * TILE_R, 256), vmem(TILE_C, 2 * TILE_R)],
        name="density",
    )(bins, area, net_box)
    ahead = [(k, k + 1) for k in range(n_rows - 1)]
    behind = [(k + 1, k) for k in range(n_rows - 1)]
    up = lax.ppermute(bottom, "rows", ahead)
    down = lax.ppermute(top, "rows", behind)
    slots, in_order, starts = pl.pallas_call(
        functools.partial(order_kernel, parts),
        out_shape=(shape(parts, 2, per, LANES), shape(rows, LANES), shape(8, LANES, dtype=jnp.int32)),
        scratch_shapes=[vmem(rows, LANES)] * 9
        + [vmem(5 * rows // 2, 2 * LANES), vmem(rows + spare, LANES), vmem(rows + spare, LANES),
           vmem(8, LANES, dtype=jnp.int32), pltpu.SMEM((8, LANES), jnp.int32), pltpu.SemaphoreType.DMA],
        cost_estimate=pl.CostEstimate(flops=15_000_000_000, bytes_accessed=2_000_000, transcendentals=0),
        name="order",
    )(owner.reshape(rows, LANES), bins, area)
    strip = jnp.concatenate([up, dens, down], axis=0)
    ahead = [(k, k + 1) for k in range(n_cols - 1)]
    behind = [(k + 1, k) for k in range(n_cols - 1)]
    left = lax.ppermute(strip[:, TILE_C - LANES :], "cols", ahead)
    right = lax.ppermute(strip[:, :LANES], "cols", behind)
    first = lax.all_to_all(slots, ("rows", "cols"), 0, 0, tiled=True)
    place = jnp.stack([lax.axis_index("rows") * TILE_R, lax.axis_index("cols") * TILE_C]).astype(jnp.int32)
    whole = pl.BlockSpec(memory_space=pltpu.VMEM)
    scalars = pl.BlockSpec(memory_space=pltpu.SMEM)
    density, shifts = pl.pallas_call(
        functools.partial(flow_kernel, parts, grid_rows, grid_cols),
        out_shape=(shape(TILE_R, TILE_C), shape(parts, 2, per, LANES)),
        in_specs=[scalars, scalars] + [whole] * 6,
        scratch_shapes=[vmem(TILE_R + 2 * EDGE, TILE_C + 2 * LANES), *[vmem(rows + spare, LANES)] * 4, vmem(2, 256, LANES)],
        cost_estimate=pl.CostEstimate(flops=15_000_000_000, bytes_accessed=2_000_000, transcendentals=0),
        name="flow",
    )(starts, place, dens, up, down, left, right, in_order)
    second = lax.all_to_all(shifts, ("rows", "cols"), 0, 0, tiled=True)
    migrated = jnp.stack([second[:, 0].reshape(-1), second[:, 1].reshape(-1), first[:, 1].reshape(-1)])
    return density, migrated, first[:, 0].reshape(-1).astype(jnp.int32)


def solution(mesh):
    both = ("rows", "cols")
    in_specs = (P(both), P(both), P(both), P(None, both))
    out_specs = (P("rows", "cols"), P(None, both), P(both))
    return jax.shard_map(on_device, mesh=mesh, in_specs=in_specs, out_specs=out_specs, check_vma=False)
```

```python
import functools
import jax
import jax.numpy as jnp
from jax import lax
from jax.experimental import pallas as pl
from jax.experimental.pallas import tpu as pltpu
from jax.sharding import PartitionSpec as P

TILE_R = 64
TILE_C = 512
DIFF_STEPS = 4
RATE = 0.2
GAMMA = 0.05
LANES = 128
EDGE = 8
DIRECT = 8
BY_DOT = 12
BF16 = jnp.bfloat16
F8 = jnp.float8_e4m3fn
SMALL = 64.0
SYMBOLS = 119
GRANT = 24 * 2 ** 20
BASE = 233
F32 = jnp.float32


def dot_nt(a, b):
    return lax.dot_general(a, b, (((1,), (1,)), ((), ())), preferred_element_type=F32)


def sublane_iota(rows, lanes=LANES):
    return lax.broadcasted_iota(jnp.int32, (rows, lanes), 0)


def narrow(x):
    return x.astype(F32).astype(BF16)


def spread(row, rows):
    lanes = row.shape[1]
    packed = jnp.broadcast_to(row, (16, lanes)).astype(BF16)
    return jnp.broadcast_to(packed[None], (rows // 16, 16, lanes)).reshape(rows, lanes)


def halves(x):
    big = x.astype(F8).astype(F32)
    return big, x - big


def expand(parts, starts_ref, total, pairs):
    per = pairs[0][2].shape[-2]
    lane = lax.broadcasted_iota(jnp.int32, (per, LANES), 1)
    place = sublane_iota(per) * LANES + lane

    def one_owner(o, carry):
        start = starts_ref[0, o]
        stop = jnp.where(o + 1 < parts, starts_ref[0, jnp.minimum(o + 1, parts - 1)], total)
        row = start // LANES
        shift = start - row * LANES
        back = lax.rem(LANES - shift, LANES)
        keep = place < stop - start
        near = lane < LANES - shift
        for source, slot, target, fill in pairs:
            a = pltpu.roll(source[pl.ds(row, per), :], back, 1)
            b = pltpu.roll(source[pl.ds(row + 1, per), :], back, 1)
            target[o, slot] = jnp.where(keep, jnp.where(near, a, b), fill)
        return carry

    lax.fori_loop(0, parts, one_owner, 0, unroll=8)


def divide(x, base):
    guess = (x.astype(F32) * (1.0 / base)).astype(jnp.int32)
    rest = x - guess * base
    guess = guess + jnp.where(rest >= base, 1, 0) - jnp.where(rest < 0, 1, 0)
    return guess, x - guess * base


def symbol(digit):
    low = digit < SYMBOLS
    j = jnp.where(low, digit, digit - SYMBOLS)
    size = jnp.left_shift(8 + (j & 7), j >> 3).astype(F32) * (1.0 / 512.0)
    return jnp.where(low, size, -size)


def digit_of(value):
    size = (jnp.abs(value) * 512.0).astype(jnp.int32)
    scale = 28 - lax.clz(size)
    j = scale * 8 + jnp.right_shift(size, scale) - 8
    return jnp.where(value < 0.0, j + SYMBOLS, j)


def area_code(area):
    return jnp.where(
        area < 1.0,
        (area - 0.5) * 256.0,
        jnp.where(area < 2.0, (area - 1.0) * 128.0 + 128.0, (area - 2.0) * 64.0 + 256.0),
    ).astype(jnp.int32)


def area_of(code):
    x = code.astype(F32)
    return jnp.where(
        x < 128.0, x * (1.0 / 256.0) + 0.5, jnp.where(x < 256.0, x * (1.0 / 128.0), x * (1.0 / 64.0) - 2.0)
    )


def placed(refs, s_ref, w_ref, first, group):
    nil = jnp.zeros((), BF16)
    one = jnp.ones((), BF16)
    s_iota = narrow(sublane_iota(LANES))
    w_iota = narrow(sublane_iota(2 * LANES))
    left, right = [], []
    for j in range(group):
        here = pl.ds(first + j, 1)
        hit = s_iota == spread(s_ref[here, :], LANES)
        left.append(
            jnp.concatenate([jnp.where(hit, spread(x[here, :], LANES), nil).astype(F8) for x in refs], axis=0)
        )
        right.append(jnp.where(w_iota == spread(w_ref[here, :], 2 * LANES), one, nil).astype(F8))
    return dot_nt(jnp.concatenate(left, axis=1), jnp.concatenate(right, axis=1))


STEPS = 8


def before(lanes):
    return narrow(sublane_iota(LANES, lanes) < lax.broadcasted_iota(jnp.int32, (LANES, lanes), 1))


def density_kernel(parts, bin_ref, area_ref, box_ref, owner_ref, dens_ref, top_ref, bottom_ref, pre_ref, cnt_ref,
                   s_ref, w_ref, a_ref, b_ref, raw_ref, cong_ref):
    all_rows = bin_ref.shape[0]
    bins = bin_ref[...]
    area = area_ref[...].astype(F32)
    s_ref[...] = (((bins >> 8) & 1) * TILE_R + (bins >> 9)).astype(F32)
    w_ref[...] = (bins & 255).astype(F32)
    a_ref[...], b_ref[...] = halves(area)
    raw_ref[...] = jnp.zeros_like(raw_ref)
    cong_ref[...] = jnp.zeros_like(cong_ref)
    nil = jnp.zeros((), BF16)
    one = jnp.ones((), BF16)
    steps = STEPS
    group = all_rows // steps
    width = box_ref.shape[1] // steps
    r_iota = narrow(sublane_iota(TILE_R, width))
    c_iota = narrow(sublane_iota(TILE_C, width) - TILE_C // 2)
    upper = before(2 * LANES)
    lane = lax.broadcasted_iota(jnp.int32, (group, LANES), 1)
    many = 8

    def step(k, carry):
        raw_ref[...] += placed((a_ref, b_ref), s_ref, w_ref, k * group, group)
        box = box_ref[:, pl.ds(pl.multiple_of(k * width, width), width)].astype(F32)
        tall = box[1:2] - box[0:1] + 1.0
        wide = box[3:4] - box[2:3] + 1.0
        weight = ((tall + wide) / (tall * wide)).astype(BF16).astype(F32)
        big, small = halves(weight)
        rows = (r_iota >= spread(box[0:1], TILE_R)) & (r_iota <= spread(box[1:2], TILE_R))
        middle = float(TILE_C // 2)
        cols = (c_iota >= spread(box[2:3] - middle, TILE_C)) & (c_iota <= spread(box[3:4] - middle, TILE_C))
        cong_ref[...] += dot_nt(
            jnp.where(cols, one, nil).astype(F8),
            jnp.concatenate(
                [jnp.where(rows, spread(x, TILE_R), nil).astype(F8) for x in (big, small * SMALL)], axis=0
            ),
        )
        here = pl.ds(pl.multiple_of(k * group, group), group)
        owner = owner_ref[here, :]
        prefix = jnp.zeros((group, LANES), F32)
        counts = jnp.zeros((group, LANES), F32)
        for g in range(0, parts, many):
            hits = [owner == g + m for m in range(many)]
            sums = jnp.dot(jnp.concatenate([narrow(h) for h in hits], axis=0), upper, preferred_element_type=F32)
            for m in range(many):
                part = sums[m * group : (m + 1) * group]
                prefix = jnp.where(hits[m], part[:, :LANES], prefix)
                counts = jnp.where(lane == g + m, part[:, LANES:], counts)
        pre_ref[here, :] = prefix
        cnt_ref[here, :] = counts
        return carry

    lax.fori_loop(0, steps, step, 0)
    raw = raw_ref[:LANES] + raw_ref[LANES:]
    raw = jnp.concatenate([raw[:TILE_R], raw[TILE_R:]], axis=1)
    cong = cong_ref[...].T
    cong = cong[:TILE_R] + cong[TILE_R:] * (1.0 / SMALL)
    dens = raw * (1.0 + GAMMA * cong)
    dens_ref[...] = dens
    top_ref[...] = dens[:EDGE]
    bottom_ref[...] = dens[TILE_R - EDGE :]


def order_kernel(parts, bin_ref, area_ref, owner_ref, pre_ref, cnt_ref, slots_ref, sorted_ref, starts_ref,
                 s_ref, w_ref, a_ref, b_ref, c_ref, acc_ref, run_bin_ref, run_area_ref, vec_ref, smem_ref, sem):
    all_rows = bin_ref.shape[0]
    group = all_rows // STEPS
    counts = cnt_ref[...]
    lower = narrow(
        lax.broadcasted_iota(jnp.int32, (all_rows, all_rows), 1)
        < lax.broadcasted_iota(jnp.int32, (all_rows, all_rows), 0)
    )
    base = jnp.dot(lower, counts.astype(BF16), preferred_element_type=F32)
    total = base[all_rows - 8 :] + counts[all_rows - 8 :]
    high = jnp.floor(total * (1.0 / 64.0))
    low = total - high * 64.0
    strict = before(LANES)
    first = jnp.dot(low.astype(BF16), strict, preferred_element_type=F32) + 64.0 * jnp.dot(
        high.astype(BF16), strict, preferred_element_type=F32
    )
    starts = jnp.broadcast_to(first[7:8], (8, LANES))
    vec_ref[...] = starts.astype(jnp.int32)
    starts_ref[...] = starts.astype(jnp.int32)
    copy = pltpu.make_async_copy(vec_ref, smem_ref, sem)
    copy.start()
    dest = (pre_ref[...] + jnp.take_along_axis(base + starts[:1], owner_ref[...], axis=1)).astype(jnp.int32)
    half = all_rows // 2
    top = jnp.where(dest >= half * LANES, 1, 0)
    s_ref[...] = ((dest >> 7) - top * half).astype(F32)
    w_ref[...] = ((dest & (LANES - 1)) + top * LANES).astype(F32)
    rest, digit = divide(area_code(area_ref[...].astype(F32)) * (TILE_R * TILE_C) + bin_ref[...], BASE)
    c_ref[...] = symbol(digit)
    rest, digit = divide(rest, BASE)
    b_ref[...] = symbol(digit)
    a_ref[...] = symbol(rest)
    acc_ref[...] = jnp.zeros_like(acc_ref)

    def place(k, carry):
        acc_ref[...] += placed((a_ref, b_ref, c_ref), s_ref, w_ref, k * group, group)
        return carry

    lax.fori_loop(0, STEPS, place, 0)
    for h in range(2):
        out = slice(h * half, (h + 1) * half)
        digits = [
            digit_of(acc_ref[k * half : (k + 1) * half, h * LANES : (h + 1) * LANES]) for k in range(3)
        ]
        code = (digits[0] * BASE + digits[1]) * BASE + digits[2]
        bins = code & (TILE_R * TILE_C - 1)
        sorted_ref[out, :] = bins
        run_bin_ref[out, :] = bins.astype(F32)
        run_area_ref[out, :] = area_of(code >> 15)
    pad = slice(all_rows, run_bin_ref.shape[0])
    run_bin_ref[pad, :] = jnp.zeros((run_bin_ref.shape[0] - all_rows, LANES), F32)
    run_area_ref[pad, :] = jnp.zeros((run_bin_ref.shape[0] - all_rows, LANES), F32)
    copy.wait()
    expand(parts, smem_ref, all_rows * LANES, ((run_bin_ref, 0, slots_ref, -1.0), (run_area_ref, 1, slots_ref, 0.0)))


def flow_kernel(parts, grid_rows, grid_cols, starts_ref, dens_in, up_ref, down_ref, left_ref, right_ref, sorted_ref,
                dens_ref, slots_ref, pad_ref, hi_ref, lo_ref, row_ref, col_ref, table_ref):
    rows = sorted_ref.shape[0]
    mid = pl.ds(EDGE, TILE_R)
    inner = pl.ds(LANES, TILE_C)
    pad_ref[mid, inner] = dens_in[...]
    pad_ref[:EDGE, inner] = up_ref[...]
    pad_ref[TILE_R + EDGE :, inner] = down_ref[...]
    pad_ref[:, :LANES] = left_ref[...]
    pad_ref[:, LANES + TILE_C :] = right_ref[...]
    tall, wide = pad_ref.shape
    grow = lax.axis_index("rows") * TILE_R + lax.broadcasted_iota(jnp.int32, (tall, 1), 0) - EDGE
    gcol = lax.axis_index("cols") * TILE_C + lax.broadcasted_iota(jnp.int32, (1, wide), 1) - LANES
    open_lower = grow + 1 != grid_rows
    open_upper = grow != 0
    open_right = gcol + 1 != grid_cols
    open_left = gcol != 0
    flow_row = jnp.zeros((TILE_R, TILE_C), F32)
    flow_col = jnp.zeros((TILE_R, TILE_C), F32)
    for step in range(DIFF_STEPS):
        d = pad_ref[...]
        lower = jnp.where(open_lower, pltpu.roll(d, tall - 1, 0) - d, 0.0)
        upper = jnp.where(open_upper, pltpu.roll(d, 1, 0) - d, 0.0)
        right = jnp.where(open_right, pltpu.roll(d, wide - 1, 1) - d, 0.0)
        left = jnp.where(open_left, pltpu.roll(d, 1, 1) - d, 0.0)
        pad_ref[...] = d + RATE * ((lower + upper) + (right + left))
        centre = (slice(EDGE, EDGE + TILE_R), slice(LANES, LANES + TILE_C))
        rate = -0.5 / (d[centre] + 1.0)
        flow_row += (lower - upper)[centre] * rate
        flow_col += (right - left)[centre] * rate
    dens_ref[...] = pad_ref[mid, inner]
    coarse, fine = [], []
    for flow in (flow_row, flow_col):
        table = jnp.concatenate([flow[:, k * LANES : (k + 1) * LANES] for k in range(TILE_C // LANES)], axis=0).T
        big = table.astype(BF16)
        coarse.append(big)
        fine.append((table - big.astype(F32)).astype(BF16))
    table = jnp.concatenate(coarse + fine, axis=0)
    bins = sorted_ref[...]
    hi_ref[:rows] = (((bins >> 7) & 3) * TILE_R + (bins >> 9)).astype(F32)
    lo_ref[:rows] = (bins & (LANES - 1)).astype(F32)
    hi_ref[rows:] = jnp.zeros((hi_ref.shape[0] - rows, LANES), F32)
    lo_ref[rows:] = jnp.zeros((hi_ref.shape[0] - rows, LANES), F32)
    hi_iota = narrow(sublane_iota(256))
    lo_iota = sublane_iota(LANES).astype(F32)
    nil = jnp.zeros((), BF16)
    one = jnp.ones((), BF16)
    for k in range(TILE_C // LANES):
        cols = slice(k * LANES, (k + 1) * LANES)
        out = slice(k * TILE_R, (k + 1) * TILE_R)
        table_ref[0, out, :] = flow_row[:, cols]
        table_ref[1, out, :] = flow_col[:, cols]

    def look_up(step, carry):
        first = step * (DIRECT + BY_DOT)
        here = pl.ds(first, DIRECT)
        row_here, lane_here = hi_ref[here, :], lo_ref[here, :].astype(jnp.int32)
        got = [jnp.zeros((DIRECT, LANES), F32)] * 2
        for k in range(table_ref.shape[1]):
            hit = row_here == float(k)
            for c in range(2):
                line = jnp.broadcast_to(table_ref[c, k : k + 1, :], (DIRECT, LANES))
                near = jnp.take_along_axis(line, lane_here, axis=1, mode="promise_in_bounds")
                got[c] = jnp.where(hit, near, got[c])
        row_ref[here, :] = got[0]
        col_ref[here, :] = got[1]
        picks = jnp.concatenate(
            [
                jnp.where(hi_iota == spread(hi_ref[pl.ds(first + DIRECT + k, 1), :], 256), one, nil)
                for k in range(BY_DOT)
            ],
            axis=1,
        )
        found = jnp.dot(table, picks, preferred_element_type=F32)
        for k in range(BY_DOT):
            here = pl.ds(first + DIRECT + k, 1)
            hit = lo_iota == lo_ref[here, :]
            part = found[:, k * LANES : (k + 1) * LANES]
            both = part[: 2 * LANES] + part[2 * LANES :]
            row_ref[here, :] = jnp.sum(jnp.where(hit, both[:LANES], 0.0), axis=0, keepdims=True)
            col_ref[here, :] = jnp.sum(jnp.where(hit, both[LANES:], 0.0), axis=0, keepdims=True)
        return carry

    lax.fori_loop(0, -(-rows // (DIRECT + BY_DOT)), look_up, 0)
    pad = slice(rows, row_ref.shape[0])
    row_ref[pad, :] = jnp.zeros((row_ref.shape[0] - rows, LANES), F32)
    col_ref[pad, :] = jnp.zeros((row_ref.shape[0] - rows, LANES), F32)
    expand(parts, starts_ref, rows * LANES, ((row_ref, 0, slots_ref, 0.0), (col_ref, 1, slots_ref, 0.0)))


def merge_kernel(first_ref, second_ref, out_ref, bin_ref):
    parts, _, per, _ = first_ref.shape

    def one_source(k, carry):
        bin_ref[pl.ds(pl.multiple_of(k * per, per), per), :] = first_ref[k, 0].astype(jnp.int32)
        for r in range(per):
            row = slice(r, r + 1)
            cells = jnp.concatenate([second_ref[k, 0, row, :], second_ref[k, 1, row, :], first_ref[k, 1, row, :]], axis=0)
            out_ref[:, pl.ds(pl.multiple_of((k * per + r) * LANES, LANES), LANES)] = cells
        return carry

    lax.fori_loop(0, parts, one_source, 0)


def shape(*dims, dtype=F32):
    return jax.ShapeDtypeStruct(dims, dtype)


def vmem(*dims, dtype=F32):
    return pltpu.VMEM(dims, dtype)


def on_device(cell_bin, cell_area, owner, net_box):
    parts = lax.axis_size(("rows", "cols"))
    count = cell_bin.shape[0]
    rows = count // LANES
    capacity = 2 * count // parts
    per = capacity // LANES
    spare = -(-max(per + 1, -rows % (DIRECT + BY_DOT)) // 8) * 8
    bins = cell_bin.reshape(rows, LANES)
    area = cell_area.reshape(rows, LANES)
    n_rows, n_cols = lax.axis_size("rows"), lax.axis_size("cols")
    grid_rows, grid_cols = n_rows * TILE_R, n_cols * TILE_C
    owner = owner.reshape(rows, LANES)
    cells = vmem(rows, LANES)
    runs = vmem(rows + spare, LANES)
    table = shape(rows, LANES)
    grant = pltpu.CompilerParams(vmem_limit_bytes=GRANT)
    dens, top, bottom, prefix, counts = pl.pallas_call(
        functools.partial(density_kernel, parts),
        out_shape=(shape(TILE_R, TILE_C), shape(EDGE, TILE_C), shape(EDGE, TILE_C), table, table),
        scratch_shapes=[cells] * 4 + [vmem(2 * LANES, 2 * LANES), vmem(TILE_C, 2 * TILE_R)],
        name="density",
    )(bins, area, net_box, owner)
    ahead = [(k, k + 1) for k in range(n_rows - 1)]
    behind = [(k + 1, k) for k in range(n_rows - 1)]
    up = lax.ppermute(bottom, "rows", ahead)
    down = lax.ppermute(top, "rows", behind)
    slots, in_order, starts = pl.pallas_call(
        functools.partial(order_kernel, parts),
        out_shape=(shape(parts, 2, per, LANES), shape(rows, LANES, dtype=jnp.int32), shape(8, LANES, dtype=jnp.int32)),
        scratch_shapes=[cells] * 5 + [vmem(3 * LANES, 2 * LANES), runs, runs]
        + [vmem(8, LANES, dtype=jnp.int32), pltpu.SMEM((8, LANES), jnp.int32), pltpu.SemaphoreType.DMA],
        compiler_params=grant,
        cost_estimate=pl.CostEstimate(flops=15_000_000_000, bytes_accessed=2_000_000, transcendentals=0),
        name="order",
    )(bins, area, owner, prefix, counts)
    up, down, slots = lax.optimization_barrier((up, down, slots))
    strip = jnp.concatenate([up, dens, down], axis=0)
    ahead = [(k, k + 1) for k in range(n_cols - 1)]
    behind = [(k + 1, k) for k in range(n_cols - 1)]
    left = lax.ppermute(strip[:, TILE_C - LANES :], "cols", ahead)
    right = lax.ppermute(strip[:, :LANES], "cols", behind)
    first = lax.all_to_all(slots, ("rows", "cols"), 0, 0, tiled=True)
    scalars = pl.BlockSpec(memory_space=pltpu.SMEM)
    density, shifts = pl.pallas_call(
        functools.partial(flow_kernel, parts, grid_rows, grid_cols),
        out_shape=(shape(TILE_R, TILE_C), shape(parts, 2, per, LANES)),
        in_specs=[scalars] + [pl.BlockSpec()] * 6,
        scratch_shapes=[vmem(TILE_R + 2 * EDGE, TILE_C + 2 * LANES), *[vmem(rows + spare, LANES)] * 4, vmem(2, 256, LANES)],
        compiler_params=grant,
        cost_estimate=pl.CostEstimate(flops=15_000_000_000, bytes_accessed=2_000_000, transcendentals=0),
        name="flow",
    )(starts, dens, up, down, left, right, in_order)
    second = lax.all_to_all(shifts, ("rows", "cols"), 0, 0, tiled=True)
    if per % 8:
        migrated = jnp.stack([second[:, 0].reshape(-1), second[:, 1].reshape(-1), first[:, 1].reshape(-1)])
        return density, migrated, first[:, 0].reshape(-1).astype(jnp.int32)
    migrated, migrated_bin = pl.pallas_call(
        merge_kernel,
        out_shape=(shape(3, parts * capacity), shape(parts * per, LANES, dtype=jnp.int32)),
        compiler_params=grant,
        name="merge",
    )(first, second)
    return density, migrated, migrated_bin.reshape(-1)


def solution(mesh):
    both = ("rows", "cols")
    in_specs = (P(both), P(both), P(both), P(None, both))
    out_specs = (P("rows", "cols"), P(None, both), P(both))
    return jax.shard_map(on_device, mesh=mesh, in_specs=in_specs, out_specs=out_specs, check_vma=False)
```

```python
import functools
import jax
import jax.numpy as jnp
from jax import lax
from jax.experimental import pallas as pl
from jax.experimental.pallas import tpu as pltpu
from jax.sharding import PartitionSpec as P

TILE_R = 64
TILE_C = 512
DIFF_STEPS = 4
RATE = 0.2
GAMMA = 0.05
LANES = 128
EDGE = 8
DIRECT = 8
BY_DOT = 16
BF16 = jnp.bfloat16
F8 = jnp.float8_e4m3fn
SMALL = 64.0
SYMBOLS = 119
GRANT = 24 * 2 ** 20
FULL = 62 * 2 ** 20
BASE = 233
F32 = jnp.float32


def dot_nt(a, b):
    return lax.dot_general(a, b, (((1,), (1,)), ((), ())), preferred_element_type=F32)


def sublane_iota(rows, lanes=LANES):
    return lax.broadcasted_iota(jnp.int32, (rows, lanes), 0)


def narrow(x):
    return x.astype(F32).astype(BF16)


def spread(row, rows):
    lanes = row.shape[1]
    packed = jnp.broadcast_to(row, (16, lanes)).astype(BF16)
    return jnp.broadcast_to(packed[None], (rows // 16, 16, lanes)).reshape(rows, lanes)


def halves(x):
    big = x.astype(F8).astype(F32)
    return big, x - big


def expand(parts, starts_ref, total, pairs):
    per = pairs[0][2].shape[-2]
    lane = lax.broadcasted_iota(jnp.int32, (per, LANES), 1)
    place = sublane_iota(per) * LANES + lane

    def one_owner(o, carry):
        start = starts_ref[0, o]
        stop = jnp.where(o + 1 < parts, starts_ref[0, jnp.minimum(o + 1, parts - 1)], total)
        row = start // LANES
        shift = start - row * LANES
        back = lax.rem(LANES - shift, LANES)
        keep = place < stop - start
        near = lane < LANES - shift
        for source, slot, target, fill in pairs:
            a = pltpu.roll(source[pl.ds(row, per), :], back, 1)
            b = pltpu.roll(source[pl.ds(row + 1, per), :], back, 1)
            target[o, slot] = jnp.where(keep, jnp.where(near, a, b), fill)
        return carry

    lax.fori_loop(0, parts, one_owner, 0, unroll=8)


def divide(x, base):
    guess = (x.astype(F32) * (1.0 / base)).astype(jnp.int32)
    rest = x - guess * base
    guess = guess + jnp.where(rest >= base, 1, 0) - jnp.where(rest < 0, 1, 0)
    return guess, x - guess * base


def symbol(digit):
    low = digit < SYMBOLS
    j = jnp.where(low, digit, digit - SYMBOLS)
    size = jnp.left_shift(8 + (j & 7), j >> 3).astype(F32) * (1.0 / 512.0)
    return jnp.where(low, size, -size)


def digit_of(value):
    size = (jnp.abs(value) * 512.0).astype(jnp.int32)
    scale = 28 - lax.clz(size)
    j = scale * 8 + jnp.right_shift(size, scale) - 8
    return jnp.where(value < 0.0, j + SYMBOLS, j)


def area_code(area):
    return jnp.where(
        area < 1.0,
        (area - 0.5) * 256.0,
        jnp.where(area < 2.0, (area - 1.0) * 128.0 + 128.0, (area - 2.0) * 64.0 + 256.0),
    ).astype(jnp.int32)


def area_of(code):
    x = code.astype(F32)
    return jnp.where(
        x < 128.0, x * (1.0 / 256.0) + 0.5, jnp.where(x < 256.0, x * (1.0 / 128.0), x * (1.0 / 64.0) - 2.0)
    )


def same(iota, row):
    rows, lanes = iota.shape
    packed = jnp.broadcast_to(row, (32, lanes)).astype(jnp.int8)
    return iota == jnp.broadcast_to(packed[None], (rows // 32, 32, lanes)).reshape(rows, lanes)


def spread8(row, rows):
    lanes = row.shape[1]
    packed = jnp.broadcast_to(row, (32, lanes)).astype(F8)
    return jnp.broadcast_to(packed[None], (rows // 32, 32, lanes)).reshape(rows, lanes)


def placed(refs, s_ref, w_ref, first, group):
    nil = jnp.zeros((), F8)
    one = jnp.ones((), F8)
    s_iota = sublane_iota(LANES).astype(jnp.int8)
    w_iota = (sublane_iota(2 * LANES) - LANES).astype(jnp.int8)
    left, right = [], []
    for j in range(group):
        here = pl.ds(first + j, 1)
        hit = same(s_iota, s_ref[here, :])
        left.append(jnp.concatenate([jnp.where(hit, spread8(x[here, :], LANES), nil) for x in refs], axis=0))
        right.append(jnp.where(same(w_iota, w_ref[here, :]), one, nil))
    return dot_nt(jnp.concatenate(left, axis=1), jnp.concatenate(right, axis=1))


STEPS = 8


def before(lanes):
    return narrow(sublane_iota(LANES, lanes) < lax.broadcasted_iota(jnp.int32, (LANES, lanes), 1))


def density_kernel(parts, bin_hbm, area_hbm, box_hbm, owner_hbm, dens_ref, top_ref, bottom_ref, starts_ref, s_ref, w_ref,
                   a_ref, b_ref, bin_ref, area_ref, box_ref, owner_ref, pre_ref, cnt_ref, raw_ref, cong_ref, sem):
    pairs = ((bin_hbm, bin_ref), (area_hbm, area_ref), (box_hbm, box_ref), (owner_hbm, owner_ref))
    copies = [pltpu.make_async_copy(x, y, sem.at[k]) for k, (x, y) in enumerate(pairs)]
    for copy in copies:
        copy.start()
    raw_ref[...] = jnp.zeros_like(raw_ref)
    cong_ref[...] = jnp.zeros_like(cong_ref)
    copies[0].wait()
    copies[1].wait()
    all_rows = bin_ref.shape[0]
    bins = bin_ref[...]
    area = area_ref[...].astype(F32)
    s_ref[...] = ((bins >> 8) & 1) * TILE_R + (bins >> 9)
    w_ref[...] = (bins & 255) - LANES
    a_ref[...], b_ref[...] = halves(area)
    copies[2].wait()
    copies[3].wait()
    nil = jnp.zeros((), BF16)
    one = jnp.ones((), BF16)
    steps = STEPS
    group = all_rows // steps
    width = box_ref.shape[1] // steps
    r_iota = narrow(sublane_iota(TILE_R, width))
    c_iota = narrow(sublane_iota(TILE_C, width) - TILE_C // 2)
    upper = before(2 * LANES).astype(F8)
    nil8 = jnp.zeros((), F8)
    one8 = jnp.ones((), F8)
    lane = lax.broadcasted_iota(jnp.int32, (group, LANES), 1)
    many = 8

    def step(k, carry):
        raw_ref[...] += placed((a_ref, b_ref), s_ref, w_ref, k * group, group)
        box = box_ref[:, pl.ds(pl.multiple_of(k * width, width), width)].astype(F32)
        tall = box[1:2] - box[0:1] + 1.0
        wide = box[3:4] - box[2:3] + 1.0
        weight = ((tall + wide) / (tall * wide)).astype(BF16).astype(F32)
        big, small = halves(weight)
        rows = (r_iota >= spread(box[0:1], TILE_R)) & (r_iota <= spread(box[1:2], TILE_R))
        middle = float(TILE_C // 2)
        cols = (c_iota >= spread(box[2:3] - middle, TILE_C)) & (c_iota <= spread(box[3:4] - middle, TILE_C))
        cong_ref[...] += dot_nt(
            jnp.where(cols, one, nil).astype(F8),
            jnp.concatenate(
                [jnp.where(rows, spread(x, TILE_R), nil).astype(F8) for x in (big, small * SMALL)], axis=0
            ),
        )
        here = pl.ds(pl.multiple_of(k * group, group), group)
        owner = owner_ref[here, :]
        owner8 = owner.astype(jnp.int8)
        prefix = jnp.zeros((group, LANES), F32)
        counts = jnp.zeros((group, LANES), F32)
        for g in range(0, parts, many):
            hits = [owner == g + m for m in range(many)]
            masks = [jnp.where(owner8 == jnp.int8(g + m), one8, nil8) for m in range(many)]
            sums = jnp.dot(jnp.concatenate(masks, axis=0), upper, preferred_element_type=F32)
            for m in range(many):
                part = sums[m * group : (m + 1) * group]
                prefix = jnp.where(hits[m], part[:, :LANES], prefix)
                counts = jnp.where(lane == g + m, part[:, LANES:], counts)
        pre_ref[here, :] = prefix
        cnt_ref[here, :] = counts
        return carry

    lax.fori_loop(0, steps, step, 0)
    raw = raw_ref[:LANES] + raw_ref[LANES:]
    raw = jnp.concatenate([raw[:TILE_R], raw[TILE_R:]], axis=1)
    cong = cong_ref[...].T
    cong = cong[:TILE_R] + cong[TILE_R:] * (1.0 / SMALL)
    dens = raw * (1.0 + GAMMA * cong)
    dens_ref[...] = dens
    top_ref[...] = dens[:EDGE]
    bottom_ref[...] = dens[TILE_R - EDGE :]

    counts = cnt_ref[...]
    lower = narrow(
        lax.broadcasted_iota(jnp.int32, (all_rows, all_rows), 1)
        < lax.broadcasted_iota(jnp.int32, (all_rows, all_rows), 0)
    )
    base = jnp.dot(lower, counts.astype(BF16), preferred_element_type=F32)
    total = base[all_rows - 8 :] + counts[all_rows - 8 :]
    high = jnp.floor(total * (1.0 / 64.0))
    low = total - high * 64.0
    strict = before(LANES)
    first = jnp.dot(low.astype(BF16), strict, preferred_element_type=F32) + 64.0 * jnp.dot(
        high.astype(BF16), strict, preferred_element_type=F32
    )
    starts = jnp.broadcast_to(first[7:8], (8, LANES))
    starts_ref[...] = starts.astype(jnp.int32)
    dest = (pre_ref[...] + jnp.take_along_axis(base + starts[:1], owner_ref[...], axis=1)).astype(jnp.int32)
    half = all_rows // 2
    top = jnp.where(dest >= half * LANES, 1, 0)
    s_ref[...] = (dest >> 7) - top * half
    w_ref[...] = (dest & (LANES - 1)) + top * LANES - LANES


def order_kernel(parts, starts_ref, s_ref, w_ref, bin_ref, area_ref, slots_ref, sorted_ref, a_ref, b_ref, c_ref, acc_ref, run_bin_ref, run_area_ref):
    all_rows = s_ref.shape[0]
    half = all_rows // 2
    group = all_rows // STEPS
    acc_ref[...] = jnp.zeros_like(acc_ref)

    def encode(k):
        here = pl.ds(pl.multiple_of(k * group, group), group)
        code = area_code(area_ref[here, :].astype(F32)) * (TILE_R * TILE_C) + bin_ref[here, :]
        rest, last = divide(code, BASE)
        first, middle = divide(rest, BASE)
        a_ref[here, :] = symbol(first)
        b_ref[here, :] = symbol(middle)
        c_ref[here, :] = symbol(last)

    def place(k, carry):
        acc_ref[...] += placed((a_ref, b_ref, c_ref), s_ref, w_ref, k * group, group)
        encode(lax.rem(k + 1, STEPS))
        return carry

    encode(0)

    lax.fori_loop(0, STEPS, place, 0)
    for h in range(2):
        out = slice(h * half, (h + 1) * half)
        digits = [
            digit_of(acc_ref[k * half : (k + 1) * half, h * LANES : (h + 1) * LANES]) for k in range(3)
        ]
        code = (digits[0] * BASE + digits[1]) * BASE + digits[2]
        bins = code & (TILE_R * TILE_C - 1)
        sorted_ref[out, :] = bins
        run_bin_ref[out, :] = bins.astype(F32)
        run_area_ref[out, :] = area_of(code >> 15)
    pad = slice(all_rows, run_bin_ref.shape[0])
    run_bin_ref[pad, :] = jnp.zeros((run_bin_ref.shape[0] - all_rows, LANES), F32)
    run_area_ref[pad, :] = jnp.zeros((run_bin_ref.shape[0] - all_rows, LANES), F32)
    expand(parts, starts_ref, all_rows * LANES, ((run_bin_ref, 0, slots_ref, -1.0), (run_area_ref, 1, slots_ref, 0.0)))


def flow_kernel(parts, grid_rows, grid_cols, starts_ref, dens_in, up_ref, down_ref, left_ref, right_ref, sorted_ref,
                dens_ref, slots_ref, pad_ref, hi_ref, lo_ref, row_ref, col_ref, table_ref):
    rows = sorted_ref.shape[0]
    mid = pl.ds(EDGE, TILE_R)
    inner = pl.ds(LANES, TILE_C)
    pad_ref[mid, inner] = dens_in[...]
    pad_ref[:EDGE, inner] = up_ref[...]
    pad_ref[TILE_R + EDGE :, inner] = down_ref[...]
    pad_ref[:, :LANES] = left_ref[...]
    pad_ref[:, LANES + TILE_C :] = right_ref[...]
    tall, wide = pad_ref.shape
    grow = lax.axis_index("rows") * TILE_R + lax.broadcasted_iota(jnp.int32, (tall, 1), 0) - EDGE
    gcol = lax.axis_index("cols") * TILE_C + lax.broadcasted_iota(jnp.int32, (1, wide), 1) - LANES
    open_lower = grow + 1 != grid_rows
    open_upper = grow != 0
    open_right = gcol + 1 != grid_cols
    open_left = gcol != 0
    flow_row = jnp.zeros((TILE_R, TILE_C), F32)
    flow_col = jnp.zeros((TILE_R, TILE_C), F32)
    for step in range(DIFF_STEPS):
        d = pad_ref[...]
        lower = jnp.where(open_lower, pltpu.roll(d, tall - 1, 0) - d, 0.0)
        upper = jnp.where(open_upper, pltpu.roll(d, 1, 0) - d, 0.0)
        right = jnp.where(open_right, pltpu.roll(d, wide - 1, 1) - d, 0.0)
        left = jnp.where(open_left, pltpu.roll(d, 1, 1) - d, 0.0)
        pad_ref[...] = d + RATE * ((lower + upper) + (right + left))
        centre = (slice(EDGE, EDGE + TILE_R), slice(LANES, LANES + TILE_C))
        rate = -0.5 / (d[centre] + 1.0)
        flow_row += (lower - upper)[centre] * rate
        flow_col += (right - left)[centre] * rate
    dens_ref[...] = pad_ref[mid, inner]
    coarse, fine = [], []
    for flow in (flow_row, flow_col):
        table = jnp.concatenate([flow[:, k * LANES : (k + 1) * LANES] for k in range(TILE_C // LANES)], axis=0).T
        big = table.astype(BF16)
        coarse.append(big)
        fine.append((table - big.astype(F32)).astype(BF16))
    table = jnp.concatenate(coarse + fine, axis=0)
    bins = sorted_ref[...]
    hi_ref[:rows] = (((bins >> 7) & 3) * TILE_R + (bins >> 9)).astype(F32)
    lo_ref[:rows] = (bins & (LANES - 1)).astype(F32)
    hi_ref[rows:] = jnp.zeros((hi_ref.shape[0] - rows, LANES), F32)
    lo_ref[rows:] = jnp.zeros((hi_ref.shape[0] - rows, LANES), F32)
    hi_iota = narrow(sublane_iota(256))
    lo_iota = sublane_iota(LANES).astype(F32)
    nil = jnp.zeros((), BF16)
    one = jnp.ones((), BF16)
    for k in range(TILE_C // LANES):
        cols = slice(k * LANES, (k + 1) * LANES)
        out = slice(k * TILE_R, (k + 1) * TILE_R)
        table_ref[0, out, :] = flow_row[:, cols]
        table_ref[1, out, :] = flow_col[:, cols]

    def look_up(step, carry):
        first = step * (DIRECT + BY_DOT)
        here = pl.ds(first, DIRECT)
        row_here, lane_here = hi_ref[here, :], lo_ref[here, :].astype(jnp.int32)
        got = [jnp.zeros((DIRECT, LANES), F32)] * 2
        for k in range(table_ref.shape[1]):
            hit = row_here == float(k)
            for c in range(2):
                line = jnp.broadcast_to(table_ref[c, k : k + 1, :], (DIRECT, LANES))
                near = jnp.take_along_axis(line, lane_here, axis=1, mode="promise_in_bounds")
                got[c] = jnp.where(hit, near, got[c])
        row_ref[here, :] = got[0]
        col_ref[here, :] = got[1]
        picks = jnp.concatenate(
            [
                jnp.where(hi_iota == spread(hi_ref[pl.ds(first + DIRECT + k, 1), :], 256), one, nil)
                for k in range(BY_DOT)
            ],
            axis=1,
        )
        found = jnp.dot(table, picks, preferred_element_type=F32)
        for k in range(BY_DOT):
            here = pl.ds(first + DIRECT + k, 1)
            hit = lo_iota == lo_ref[here, :]
            part = found[:, k * LANES : (k + 1) * LANES]
            both = part[: 2 * LANES] + part[2 * LANES :]
            row_ref[here, :] = jnp.sum(jnp.where(hit, both[:LANES], 0.0), axis=0, keepdims=True)
            col_ref[here, :] = jnp.sum(jnp.where(hit, both[LANES:], 0.0), axis=0, keepdims=True)
        return carry

    lax.fori_loop(0, -(-rows // (DIRECT + BY_DOT)), look_up, 0)
    pad = slice(rows, row_ref.shape[0])
    row_ref[pad, :] = jnp.zeros((row_ref.shape[0] - rows, LANES), F32)
    col_ref[pad, :] = jnp.zeros((row_ref.shape[0] - rows, LANES), F32)
    expand(parts, starts_ref, rows * LANES, ((row_ref, 0, slots_ref, 0.0), (col_ref, 1, slots_ref, 0.0)))


def merge_kernel(first_ref, second_ref, out_ref, bin_ref):
    parts, _, per, _ = first_ref.shape

    def one_source(k, carry):
        bin_ref[pl.ds(pl.multiple_of(k * per, per), per), :] = first_ref[k, 0].astype(jnp.int32)
        for r in range(per):
            row = slice(r, r + 1)
            cells = jnp.concatenate([second_ref[k, 0, row, :], second_ref[k, 1, row, :], first_ref[k, 1, row, :]], axis=0)
            out_ref[:, pl.ds(pl.multiple_of((k * per + r) * LANES, LANES), LANES)] = cells
        return carry

    lax.fori_loop(0, parts, one_source, 0)


def shape(*dims, dtype=F32):
    return jax.ShapeDtypeStruct(dims, dtype)


def vmem(*dims, dtype=F32):
    return pltpu.VMEM(dims, dtype)


def on_device(cell_bin, cell_area, owner, net_box):
    parts = lax.axis_size(("rows", "cols"))
    count = cell_bin.shape[0]
    rows = count // LANES
    capacity = 2 * count // parts
    per = capacity // LANES
    spare = -(-max(per + 1, -rows % (DIRECT + BY_DOT)) // 8) * 8
    bins = cell_bin.reshape(rows, LANES)
    area = cell_area.reshape(rows, LANES)
    n_rows, n_cols = lax.axis_size("rows"), lax.axis_size("cols")
    grid_rows, grid_cols = n_rows * TILE_R, n_cols * TILE_C
    owner = owner.reshape(rows, LANES)
    cells = vmem(rows, LANES)
    runs = vmem(rows + spare, LANES)
    table = shape(rows, LANES)
    grant = pltpu.CompilerParams(vmem_limit_bytes=GRANT)
    whole_ints = shape(rows, LANES, dtype=jnp.int32)
    int_cells = vmem(rows, LANES, dtype=jnp.int32)
    dens, top, bottom, starts, s, w = pl.pallas_call(
        functools.partial(density_kernel, parts),
        out_shape=(shape(TILE_R, TILE_C), shape(EDGE, TILE_C), shape(EDGE, TILE_C), shape(8, LANES, dtype=jnp.int32),
                   whole_ints, whole_ints),
        in_specs=[pl.BlockSpec(memory_space=pltpu.HBM)] * 4,
        scratch_shapes=[cells, cells, int_cells, vmem(rows, LANES, dtype=BF16), vmem(*net_box.shape, dtype=jnp.int32), int_cells, cells, cells,
                        vmem(2 * LANES, 2 * LANES), vmem(TILE_C, 2 * TILE_R), pltpu.SemaphoreType.DMA((4,))],
        compiler_params=pltpu.CompilerParams(vmem_limit_bytes=FULL),
        name="density",
    )(bins, area, net_box, owner)
    ahead = [(k, k + 1) for k in range(n_rows - 1)]
    behind = [(k + 1, k) for k in range(n_rows - 1)]
    up = lax.ppermute(bottom, "rows", ahead)
    down = lax.ppermute(top, "rows", behind)
    scalars = pl.BlockSpec(memory_space=pltpu.SMEM)
    slots, in_order = pl.pallas_call(
        functools.partial(order_kernel, parts),
        out_shape=(shape(parts, 2, per, LANES), whole_ints),
        in_specs=[scalars] + [pl.BlockSpec()] * 4,
        scratch_shapes=[cells, cells, cells, vmem(3 * LANES, 2 * LANES), runs, runs],
        compiler_params=pltpu.CompilerParams(vmem_limit_bytes=FULL),
        cost_estimate=pl.CostEstimate(flops=15_000_000_000, bytes_accessed=2_000_000, transcendentals=0),
        name="order",
    )(starts, s, w, bins, area)
    up, down, slots = lax.optimization_barrier((up, down, slots))
    strip = jnp.concatenate([up, dens, down], axis=0)
    ahead = [(k, k + 1) for k in range(n_cols - 1)]
    behind = [(k + 1, k) for k in range(n_cols - 1)]
    left = lax.ppermute(strip[:, TILE_C - LANES :], "cols", ahead)
    right = lax.ppermute(strip[:, :LANES], "cols", behind)
    first = lax.all_to_all(slots, ("rows", "cols"), 0, 0, tiled=True)
    density, shifts = pl.pallas_call(
        functools.partial(flow_kernel, parts, grid_rows, grid_cols),
        out_shape=(shape(TILE_R, TILE_C), shape(parts, 2, per, LANES)),
        in_specs=[scalars] + [pl.BlockSpec()] * 6,
        scratch_shapes=[vmem(TILE_R + 2 * EDGE, TILE_C + 2 * LANES), *[vmem(rows + spare, LANES)] * 4, vmem(2, 256, LANES)],
        compiler_params=grant,
        cost_estimate=pl.CostEstimate(flops=15_000_000_000, bytes_accessed=2_000_000, transcendentals=0),
        name="flow",
    )(starts, dens, up, down, left, right, in_order)
    second = lax.all_to_all(shifts, ("rows", "cols"), 0, 0, tiled=True)
    if per % 8:
        migrated = jnp.stack([second[:, 0].reshape(-1), second[:, 1].reshape(-1), first[:, 1].reshape(-1)])
        return density, migrated, first[:, 0].reshape(-1).astype(jnp.int32)
    migrated, migrated_bin = pl.pallas_call(
        merge_kernel,
        out_shape=(shape(3, parts * capacity), shape(parts * per, LANES, dtype=jnp.int32)),
        compiler_params=grant,
        name="merge",
    )(first, second)
    return density, migrated, migrated_bin.reshape(-1)


def solution(mesh):
    both = ("rows", "cols")
    in_specs = (P(both), P(both), P(both), P(None, both))
    out_specs = (P("rows", "cols"), P(None, both), P(both))
    return jax.shard_map(on_device, mesh=mesh, in_specs=in_specs, out_specs=out_specs, check_vma=False)
```

```python
import functools
import jax
import jax.numpy as jnp
from jax import lax
from jax.experimental import pallas as pl
from jax.experimental.pallas import tpu as pltpu
from jax.sharding import PartitionSpec as P

TILE_R = 64
TILE_C = 512
DIFF_STEPS = 4
RATE = 0.2
GAMMA = 0.05
LANES = 128
EDGE = 8
DIRECT = 8
BY_DOT = 16
BF16 = jnp.bfloat16
F8 = jnp.float8_e4m3fn
SMALL = 64.0
SYMBOLS = 119
GRANT = 24 * 2 ** 20
FULL = 62 * 2 ** 20
BASE = 233
F32 = jnp.float32


def dot_nt(a, b):
    return lax.dot_general(a, b, (((1,), (1,)), ((), ())), preferred_element_type=F32)


def sublane_iota(rows, lanes=LANES):
    return lax.broadcasted_iota(jnp.int32, (rows, lanes), 0)


def narrow(x):
    return x.astype(F32).astype(BF16)


def spread(row, rows):
    lanes = row.shape[1]
    packed = jnp.broadcast_to(row, (16, lanes)).astype(BF16)
    return jnp.broadcast_to(packed[None], (rows // 16, 16, lanes)).reshape(rows, lanes)


def halves(x):
    big = x.astype(F8).astype(F32)
    return big, x - big


def expand(parts, starts_ref, total, pairs):
    per = pairs[0][2].shape[-2]
    lane = lax.broadcasted_iota(jnp.int32, (per, LANES), 1)
    place = sublane_iota(per) * LANES + lane

    def one_owner(o, carry):
        start = starts_ref[0, o]
        stop = jnp.where(o + 1 < parts, starts_ref[0, jnp.minimum(o + 1, parts - 1)], total)
        row = start // LANES
        shift = start - row * LANES
        back = lax.rem(LANES - shift, LANES)
        keep = place < stop - start
        near = lane < LANES - shift
        for source, slot, target, fill in pairs:
            a = pltpu.roll(source[pl.ds(row, per), :], back, 1)
            b = pltpu.roll(source[pl.ds(row + 1, per), :], back, 1)
            target[o, slot] = jnp.where(keep, jnp.where(near, a, b), fill)
        return carry

    lax.fori_loop(0, parts, one_owner, 0, unroll=8)


def divide(x, base):
    guess = (x.astype(F32) * (1.0 / base)).astype(jnp.int32)
    rest = x - guess * base
    guess = guess + jnp.where(rest >= base, 1, 0) - jnp.where(rest < 0, 1, 0)
    return guess, x - guess * base


def symbol(digit):
    low = digit < SYMBOLS
    j = jnp.where(low, digit, digit - SYMBOLS)
    size = jnp.left_shift(8 + (j & 7), j >> 3).astype(F32) * (1.0 / 512.0)
    return jnp.where(low, size, -size)


def digit_of(value):
    size = (jnp.abs(value) * 512.0).astype(jnp.int32)
    scale = 28 - lax.clz(size)
    j = scale * 8 + jnp.right_shift(size, scale) - 8
    return jnp.where(value < 0.0, j + SYMBOLS, j)


def area_code(area):
    return jnp.where(
        area < 1.0,
        (area - 0.5) * 256.0,
        jnp.where(area < 2.0, (area - 1.0) * 128.0 + 128.0, (area - 2.0) * 64.0 + 256.0),
    ).astype(jnp.int32)


def area_of(code):
    x = code.astype(F32)
    return jnp.where(
        x < 128.0, x * (1.0 / 256.0) + 0.5, jnp.where(x < 256.0, x * (1.0 / 128.0), x * (1.0 / 64.0) - 2.0)
    )


def same(iota, row):
    rows, lanes = iota.shape
    packed = jnp.broadcast_to(row, (32, lanes)).astype(jnp.int8)
    return iota == jnp.broadcast_to(packed[None], (rows // 32, 32, lanes)).reshape(rows, lanes)


def spread8(row, rows):
    lanes = row.shape[1]
    packed = jnp.broadcast_to(row, (32, lanes)).astype(F8)
    return jnp.broadcast_to(packed[None], (rows // 32, 32, lanes)).reshape(rows, lanes)


def placed(refs, s_ref, w_ref, first, group):
    nil = jnp.zeros((), F8)
    one = jnp.ones((), F8)
    s_iota = sublane_iota(LANES).astype(jnp.int8)
    w_iota = (sublane_iota(2 * LANES) - LANES).astype(jnp.int8)
    left, right = [], []
    for j in range(group):
        here = pl.ds(first + j, 1)
        hit = same(s_iota, s_ref[here, :])
        left.append(jnp.concatenate([jnp.where(hit, spread8(x[here, :], LANES), nil) for x in refs], axis=0))
        right.append(jnp.where(same(w_iota, w_ref[here, :]), one, nil))
    return dot_nt(jnp.concatenate(left, axis=1), jnp.concatenate(right, axis=1))


STEPS = 8


def before(lanes):
    return narrow(sublane_iota(LANES, lanes) < lax.broadcasted_iota(jnp.int32, (LANES, lanes), 1))


def density_kernel(parts, bin_hbm, area_hbm, box_hbm, owner_hbm, dens_ref, top_ref, bottom_ref, starts_ref, s_ref, w_ref, code_ref,
                   a_ref, b_ref, bin_ref, area_ref, box_ref, owner_ref, pre_ref, cnt_ref, raw_ref, cong_ref, sem):
    pairs = ((bin_hbm, bin_ref), (area_hbm, area_ref), (box_hbm, box_ref), (owner_hbm, owner_ref))
    copies = [pltpu.make_async_copy(x, y, sem.at[k]) for k, (x, y) in enumerate(pairs)]
    for copy in copies:
        copy.start()
    raw_ref[...] = jnp.zeros_like(raw_ref)
    cong_ref[...] = jnp.zeros_like(cong_ref)
    copies[0].wait()
    copies[1].wait()
    all_rows = bin_ref.shape[0]
    bins = bin_ref[...]
    area = area_ref[...].astype(F32)
    s_ref[...] = ((bins >> 8) & 1) * TILE_R + (bins >> 9)
    w_ref[...] = (bins & 255) - LANES
    a_ref[...], b_ref[...] = halves(area)
    code_ref[...] = area_code(area) * (TILE_R * TILE_C) + bins
    copies[2].wait()
    copies[3].wait()
    nil = jnp.zeros((), BF16)
    one = jnp.ones((), BF16)
    steps = STEPS
    group = all_rows // steps
    width = box_ref.shape[1] // steps
    r_iota = narrow(sublane_iota(TILE_R, width))
    c_iota = narrow(sublane_iota(TILE_C, width) - TILE_C // 2)
    upper = before(2 * LANES).astype(F8)
    nil8 = jnp.zeros((), F8)
    one8 = jnp.ones((), F8)
    lane = lax.broadcasted_iota(jnp.int32, (group, LANES), 1)
    many = 8

    def step(k, carry):
        raw_ref[...] += placed((a_ref, b_ref), s_ref, w_ref, k * group, group)
        box = box_ref[:, pl.ds(pl.multiple_of(k * width, width), width)].astype(F32)
        tall = box[1:2] - box[0:1] + 1.0
        wide = box[3:4] - box[2:3] + 1.0
        weight = ((tall + wide) / (tall * wide)).astype(BF16).astype(F32)
        big, small = halves(weight)
        rows = (r_iota >= spread(box[0:1], TILE_R)) & (r_iota <= spread(box[1:2], TILE_R))
        middle = float(TILE_C // 2)
        cols = (c_iota >= spread(box[2:3] - middle, TILE_C)) & (c_iota <= spread(box[3:4] - middle, TILE_C))
        cong_ref[...] += dot_nt(
            jnp.where(cols, one, nil).astype(F8),
            jnp.concatenate(
                [jnp.where(rows, spread(x, TILE_R), nil).astype(F8) for x in (big, small * SMALL)], axis=0
            ),
        )
        here = pl.ds(pl.multiple_of(k * group, group), group)
        owner = owner_ref[here, :]
        owner8 = owner.astype(jnp.int8)
        prefix = jnp.zeros((group, LANES), F32)
        counts = jnp.zeros((group, LANES), F32)
        for g in range(0, parts, many):
            hits = [owner == g + m for m in range(many)]
            masks = [jnp.where(owner8 == jnp.int8(g + m), one8, nil8) for m in range(many)]
            sums = jnp.dot(jnp.concatenate(masks, axis=0), upper, preferred_element_type=F32)
            for m in range(many):
                part = sums[m * group : (m + 1) * group]
                prefix = jnp.where(hits[m], part[:, :LANES], prefix)
                counts = jnp.where(lane == g + m, part[:, LANES:], counts)
        pre_ref[here, :] = prefix
        cnt_ref[here, :] = counts
        return carry

    lax.fori_loop(0, steps, step, 0)
    raw = raw_ref[:LANES] + raw_ref[LANES:]
    raw = jnp.concatenate([raw[:TILE_R], raw[TILE_R:]], axis=1)
    cong = cong_ref[...].T
    cong = cong[:TILE_R] + cong[TILE_R:] * (1.0 / SMALL)
    dens = raw * (1.0 + GAMMA * cong)
    dens_ref[...] = dens
    top_ref[...] = dens[:EDGE]
    bottom_ref[...] = dens[TILE_R - EDGE :]

    counts = cnt_ref[...]
    lower = narrow(
        lax.broadcasted_iota(jnp.int32, (all_rows, all_rows), 1)
        < lax.broadcasted_iota(jnp.int32, (all_rows, all_rows), 0)
    )
    base = jnp.dot(lower, counts.astype(BF16), preferred_element_type=F32)
    total = base[all_rows - 8 :] + counts[all_rows - 8 :]
    high = jnp.floor(total * (1.0 / 64.0))
    low = total - high * 64.0
    strict = before(LANES)
    first = jnp.dot(low.astype(BF16), strict, preferred_element_type=F32) + 64.0 * jnp.dot(
        high.astype(BF16), strict, preferred_element_type=F32
    )
    starts = jnp.broadcast_to(first[7:8], (8, LANES))
    starts_ref[...] = starts.astype(jnp.int32)
    dest = (pre_ref[...] + jnp.take_along_axis(base + starts[:1], owner_ref[...], axis=1)).astype(jnp.int32)
    half = all_rows // 2
    top = jnp.where(dest >= half * LANES, 1, 0)
    s_ref[...] = (dest >> 7) - top * half
    w_ref[...] = (dest & (LANES - 1)) + top * LANES - LANES


def order_kernel(parts, starts_ref, s_ref, w_ref, code_ref, slots_ref, sorted_ref, a_ref, b_ref, c_ref, acc_ref, run_bin_ref, run_area_ref):
    all_rows = s_ref.shape[0]
    half = all_rows // 2
    group = all_rows // STEPS
    acc_ref[...] = jnp.zeros_like(acc_ref)

    def encode(k):
        here = pl.ds(pl.multiple_of(k * group, group), group)
        rest, last = divide(code_ref[here, :], BASE)
        first, middle = divide(rest, BASE)
        a_ref[here, :] = symbol(first)
        b_ref[here, :] = symbol(middle)
        c_ref[here, :] = symbol(last)

    def place(k, carry):
        acc_ref[...] += placed((a_ref, b_ref, c_ref), s_ref, w_ref, k * group, group)
        encode(lax.rem(k + 1, STEPS))
        return carry

    encode(0)

    lax.fori_loop(0, STEPS, place, 0)
    for h in range(2):
        out = slice(h * half, (h + 1) * half)
        digits = [
            digit_of(acc_ref[k * half : (k + 1) * half, h * LANES : (h + 1) * LANES]) for k in range(3)
        ]
        code = (digits[0] * BASE + digits[1]) * BASE + digits[2]
        bins = code & (TILE_R * TILE_C - 1)
        sorted_ref[out, :] = bins
        run_bin_ref[out, :] = bins.astype(F32)
        run_area_ref[out, :] = area_of(code >> 15)
    pad = slice(all_rows, run_bin_ref.shape[0])
    run_bin_ref[pad, :] = jnp.zeros((run_bin_ref.shape[0] - all_rows, LANES), F32)
    run_area_ref[pad, :] = jnp.zeros((run_bin_ref.shape[0] - all_rows, LANES), F32)
    expand(parts, starts_ref, all_rows * LANES, ((run_bin_ref, 0, slots_ref, -1.0), (run_area_ref, 1, slots_ref, 0.0)))


def flow_kernel(parts, grid_rows, grid_cols, starts_ref, dens_in, up_ref, down_ref, left_ref, right_ref, sorted_ref,
                dens_ref, slots_ref, pad_ref, hi_ref, lo_ref, row_ref, col_ref, table_ref):
    rows = sorted_ref.shape[0]
    mid = pl.ds(EDGE, TILE_R)
    inner = pl.ds(LANES, TILE_C)
    pad_ref[mid, inner] = dens_in[...]
    pad_ref[:EDGE, inner] = up_ref[...]
    pad_ref[TILE_R + EDGE :, inner] = down_ref[...]
    pad_ref[:, :LANES] = left_ref[...]
    pad_ref[:, LANES + TILE_C :] = right_ref[...]
    tall, wide = pad_ref.shape
    grow = lax.axis_index("rows") * TILE_R + lax.broadcasted_iota(jnp.int32, (tall, 1), 0) - EDGE
    gcol = lax.axis_index("cols") * TILE_C + lax.broadcasted_iota(jnp.int32, (1, wide), 1) - LANES
    open_lower = grow + 1 != grid_rows
    open_upper = grow != 0
    open_right = gcol + 1 != grid_cols
    open_left = gcol != 0
    flow_row = jnp.zeros((TILE_R, TILE_C), F32)
    flow_col = jnp.zeros((TILE_R, TILE_C), F32)
    for step in range(DIFF_STEPS):
        d = pad_ref[...]
        lower = jnp.where(open_lower, pltpu.roll(d, tall - 1, 0) - d, 0.0)
        upper = jnp.where(open_upper, pltpu.roll(d, 1, 0) - d, 0.0)
        right = jnp.where(open_right, pltpu.roll(d, wide - 1, 1) - d, 0.0)
        left = jnp.where(open_left, pltpu.roll(d, 1, 1) - d, 0.0)
        pad_ref[...] = d + RATE * ((lower + upper) + (right + left))
        centre = (slice(EDGE, EDGE + TILE_R), slice(LANES, LANES + TILE_C))
        rate = -0.5 / (d[centre] + 1.0)
        flow_row += (lower - upper)[centre] * rate
        flow_col += (right - left)[centre] * rate
    dens_ref[...] = pad_ref[mid, inner]
    coarse, fine = [], []
    for flow in (flow_row, flow_col):
        table = jnp.concatenate([flow[:, k * LANES : (k + 1) * LANES] for k in range(TILE_C // LANES)], axis=0).T
        big = table.astype(BF16)
        coarse.append(big)
        fine.append((table - big.astype(F32)).astype(BF16))
    table = jnp.concatenate(coarse + fine, axis=0)
    bins = sorted_ref[...]
    hi_ref[:rows] = (((bins >> 7) & 3) * TILE_R + (bins >> 9)).astype(F32)
    lo_ref[:rows] = (bins & (LANES - 1)).astype(F32)
    hi_ref[rows:] = jnp.zeros((hi_ref.shape[0] - rows, LANES), F32)
    lo_ref[rows:] = jnp.zeros((hi_ref.shape[0] - rows, LANES), F32)
    hi_iota = narrow(sublane_iota(256))
    lo_iota = sublane_iota(LANES).astype(F32)
    nil = jnp.zeros((), BF16)
    one = jnp.ones((), BF16)
    for k in range(TILE_C // LANES):
        cols = slice(k * LANES, (k + 1) * LANES)
        out = slice(k * TILE_R, (k + 1) * TILE_R)
        table_ref[0, out, :] = flow_row[:, cols]
        table_ref[1, out, :] = flow_col[:, cols]

    def look_up(step, carry):
        first = step * (DIRECT + BY_DOT)
        here = pl.ds(first, DIRECT)
        row_here, lane_here = hi_ref[here, :], lo_ref[here, :].astype(jnp.int32)
        got = [jnp.zeros((DIRECT, LANES), F32)] * 2
        for k in range(table_ref.shape[1]):
            hit = row_here == float(k)
            for c in range(2):
                line = jnp.broadcast_to(table_ref[c, k : k + 1, :], (DIRECT, LANES))
                near = jnp.take_along_axis(line, lane_here, axis=1, mode="promise_in_bounds")
                got[c] = jnp.where(hit, near, got[c])
        row_ref[here, :] = got[0]
        col_ref[here, :] = got[1]
        picks = jnp.concatenate(
            [
                jnp.where(hi_iota == spread(hi_ref[pl.ds(first + DIRECT + k, 1), :], 256), one, nil)
                for k in range(BY_DOT)
            ],
            axis=1,
        )
        found = jnp.dot(table, picks, preferred_element_type=F32)
        for k in range(BY_DOT):
            here = pl.ds(first + DIRECT + k, 1)
            hit = lo_iota == lo_ref[here, :]
            part = found[:, k * LANES : (k + 1) * LANES]
            both = part[: 2 * LANES] + part[2 * LANES :]
            row_ref[here, :] = jnp.sum(jnp.where(hit, both[:LANES], 0.0), axis=0, keepdims=True)
            col_ref[here, :] = jnp.sum(jnp.where(hit, both[LANES:], 0.0), axis=0, keepdims=True)
        return carry

    lax.fori_loop(0, -(-rows // (DIRECT + BY_DOT)), look_up, 0)
    pad = slice(rows, row_ref.shape[0])
    row_ref[pad, :] = jnp.zeros((row_ref.shape[0] - rows, LANES), F32)
    col_ref[pad, :] = jnp.zeros((row_ref.shape[0] - rows, LANES), F32)
    expand(parts, starts_ref, rows * LANES, ((row_ref, 0, slots_ref, 0.0), (col_ref, 1, slots_ref, 0.0)))


def merge_kernel(first_ref, second_ref, out_ref, bin_ref):
    parts, _, per, _ = first_ref.shape

    def one_source(k, carry):
        bin_ref[pl.ds(pl.multiple_of(k * per, per), per), :] = first_ref[k, 0].astype(jnp.int32)
        for r in range(per):
            row = slice(r, r + 1)
            cells = jnp.concatenate([second_ref[k, 0, row, :], second_ref[k, 1, row, :], first_ref[k, 1, row, :]], axis=0)
            out_ref[:, pl.ds(pl.multiple_of((k * per + r) * LANES, LANES), LANES)] = cells
        return carry

    lax.fori_loop(0, parts, one_source, 0)


def shape(*dims, dtype=F32):
    return jax.ShapeDtypeStruct(dims, dtype)


def vmem(*dims, dtype=F32):
    return pltpu.VMEM(dims, dtype)


def on_device(cell_bin, cell_area, owner, net_box):
    parts = lax.axis_size(("rows", "cols"))
    count = cell_bin.shape[0]
    rows = count // LANES
    capacity = 2 * count // parts
    per = capacity // LANES
    spare = -(-max(per + 1, -rows % (DIRECT + BY_DOT)) // 8) * 8
    bins = cell_bin.reshape(rows, LANES)
    area = cell_area.reshape(rows, LANES)
    n_rows, n_cols = lax.axis_size("rows"), lax.axis_size("cols")
    grid_rows, grid_cols = n_rows * TILE_R, n_cols * TILE_C
    owner = owner.reshape(rows, LANES)
    cells = vmem(rows, LANES)
    runs = vmem(rows + spare, LANES)
    table = shape(rows, LANES)
    grant = pltpu.CompilerParams(vmem_limit_bytes=GRANT)
    int_cells = vmem(rows, LANES, dtype=jnp.int32)
    dens, top, bottom, starts, s, w, codes = pl.pallas_call(
        functools.partial(density_kernel, parts),
        out_shape=(vmem(TILE_R, TILE_C), vmem(EDGE, TILE_C), vmem(EDGE, TILE_C), shape(8, LANES, dtype=jnp.int32),
                   int_cells, int_cells, int_cells),
        in_specs=[pl.BlockSpec(memory_space=pltpu.HBM)] * 4,
        scratch_shapes=[cells, cells, int_cells, vmem(rows, LANES, dtype=BF16), vmem(*net_box.shape, dtype=jnp.int32), int_cells, cells, cells,
                        vmem(2 * LANES, 2 * LANES), vmem(TILE_C, 2 * TILE_R), pltpu.SemaphoreType.DMA((4,))],
        compiler_params=pltpu.CompilerParams(vmem_limit_bytes=FULL),
        name="density",
    )(bins, area, net_box, owner)
    ahead = [(k, k + 1) for k in range(n_rows - 1)]
    behind = [(k + 1, k) for k in range(n_rows - 1)]
    up = lax.ppermute(bottom, "rows", ahead)
    down = lax.ppermute(top, "rows", behind)
    scalars = pl.BlockSpec(memory_space=pltpu.SMEM)
    slots, in_order = pl.pallas_call(
        functools.partial(order_kernel, parts),
        out_shape=(vmem(parts, 2, per, LANES), int_cells),
        in_specs=[scalars] + [pl.BlockSpec()] * 3,
        scratch_shapes=[cells, cells, cells, vmem(3 * LANES, 2 * LANES), runs, runs],
        compiler_params=grant,
        cost_estimate=pl.CostEstimate(flops=15_000_000_000, bytes_accessed=2_000_000, transcendentals=0),
        name="order",
    )(starts, s, w, codes)
    up, down, slots = lax.optimization_barrier((up, down, slots))
    strip = jnp.concatenate([up, dens, down], axis=0)
    ahead = [(k, k + 1) for k in range(n_cols - 1)]
    behind = [(k + 1, k) for k in range(n_cols - 1)]
    left = lax.ppermute(strip[:, TILE_C - LANES :], "cols", ahead)
    right = lax.ppermute(strip[:, :LANES], "cols", behind)
    first = lax.all_to_all(slots, ("rows", "cols"), 0, 0, tiled=True)
    density, shifts = pl.pallas_call(
        functools.partial(flow_kernel, parts, grid_rows, grid_cols),
        out_shape=(shape(TILE_R, TILE_C), vmem(parts, 2, per, LANES)),
        in_specs=[scalars] + [pl.BlockSpec()] * 6,
        scratch_shapes=[vmem(TILE_R + 2 * EDGE, TILE_C + 2 * LANES), *[vmem(rows + spare, LANES)] * 4, vmem(2, 256, LANES)],
        compiler_params=grant,
        cost_estimate=pl.CostEstimate(flops=15_000_000_000, bytes_accessed=2_000_000, transcendentals=0),
        name="flow",
    )(starts, dens, up, down, left, right, in_order)
    second = lax.all_to_all(shifts, ("rows", "cols"), 0, 0, tiled=True)
    if per % 8:
        migrated = jnp.stack([second[:, 0].reshape(-1), second[:, 1].reshape(-1), first[:, 1].reshape(-1)])
        return density, migrated, first[:, 0].reshape(-1).astype(jnp.int32)
    migrated, migrated_bin = pl.pallas_call(
        merge_kernel,
        out_shape=(shape(3, parts * capacity), shape(parts * per, LANES, dtype=jnp.int32)),
        compiler_params=grant,
        name="merge",
    )(first, second)
    return density, migrated, migrated_bin.reshape(-1)


def solution(mesh):
    both = ("rows", "cols")
    in_specs = (P(both), P(both), P(both), P(None, both))
    out_specs = (P("rows", "cols"), P(None, both), P(both))
    return jax.shard_map(on_device, mesh=mesh, in_specs=in_specs, out_specs=out_specs, check_vma=False)
```

```python
import functools
import jax
import jax.numpy as jnp
from jax import lax
from jax.experimental import pallas as pl
from jax.experimental.pallas import tpu as pltpu
from jax.sharding import PartitionSpec as P

TILE_R = 64
TILE_C = 512
DIFF_STEPS = 4
RATE = 0.2
GAMMA = 0.05
LANES = 128
EDGE = 8
DIRECT = 8
BY_DOT = 16
BF16 = jnp.bfloat16
F8 = jnp.float8_e4m3fn
SMALL = 64.0
SYMBOLS = 119
GRANT = 24 * 2 ** 20
FULL = 62 * 2 ** 20
BASE = 233
F32 = jnp.float32


def dot_nt(a, b):
    return lax.dot_general(a, b, (((1,), (1,)), ((), ())), preferred_element_type=F32)


def sublane_iota(rows, lanes=LANES):
    return lax.broadcasted_iota(jnp.int32, (rows, lanes), 0)


def narrow(x):
    return x.astype(F32).astype(BF16)


def spread(row, rows):
    lanes = row.shape[1]
    packed = jnp.broadcast_to(row, (16, lanes)).astype(BF16)
    return jnp.broadcast_to(packed[None], (rows // 16, 16, lanes)).reshape(rows, lanes)


def halves(x):
    big = x.astype(F8).astype(F32)
    return big, x - big


def expand(parts, starts_ref, total, pairs):
    per = pairs[0][2].shape[-2]
    lane = lax.broadcasted_iota(jnp.int32, (per, LANES), 1)
    place = sublane_iota(per) * LANES + lane

    def one_owner(o, carry):
        start = starts_ref[0, o]
        stop = jnp.where(o + 1 < parts, starts_ref[0, jnp.minimum(o + 1, parts - 1)], total)
        row = start // LANES
        shift = start - row * LANES
        back = lax.rem(LANES - shift, LANES)
        keep = place < stop - start
        near = lane < LANES - shift
        for source, slot, target, fill in pairs:
            a = pltpu.roll(source[pl.ds(row, per), :], back, 1)
            b = pltpu.roll(source[pl.ds(row + 1, per), :], back, 1)
            target[o, slot] = jnp.where(keep, jnp.where(near, a, b), fill)
        return carry

    lax.fori_loop(0, parts, one_owner, 0, unroll=8)


def divide(x, base):
    guess = (x.astype(F32) * (1.0 / base)).astype(jnp.int32)
    rest = x - guess * base
    guess = guess + jnp.where(rest >= base, 1, 0) - jnp.where(rest < 0, 1, 0)
    return guess, x - guess * base


def symbol(digit):
    low = digit < SYMBOLS
    j = jnp.where(low, digit, digit - SYMBOLS)
    size = jnp.left_shift(8 + (j & 7), j >> 3).astype(F32) * (1.0 / 512.0)
    return jnp.where(low, size, -size)


def digit_of(value):
    size = (jnp.abs(value) * 512.0).astype(jnp.int32)
    scale = 28 - lax.clz(size)
    j = scale * 8 + jnp.right_shift(size, scale) - 8
    return jnp.where(value < 0.0, j + SYMBOLS, j)


def area_code(area):
    return jnp.where(
        area < 1.0,
        (area - 0.5) * 256.0,
        jnp.where(area < 2.0, (area - 1.0) * 128.0 + 128.0, (area - 2.0) * 64.0 + 256.0),
    ).astype(jnp.int32)


def area_of(code):
    x = code.astype(F32)
    return jnp.where(
        x < 128.0, x * (1.0 / 256.0) + 0.5, jnp.where(x < 256.0, x * (1.0 / 128.0), x * (1.0 / 64.0) - 2.0)
    )


def same(iota, row):
    rows, lanes = iota.shape
    packed = jnp.broadcast_to(row, (32, lanes)).astype(jnp.int8)
    return iota == jnp.broadcast_to(packed[None], (rows // 32, 32, lanes)).reshape(rows, lanes)


def spread8(row, rows):
    lanes = row.shape[1]
    packed = jnp.broadcast_to(row, (32, lanes)).astype(F8)
    return jnp.broadcast_to(packed[None], (rows // 32, 32, lanes)).reshape(rows, lanes)


def placed(refs, s_ref, w_ref, first, group):
    nil = jnp.zeros((), F8)
    one = jnp.ones((), F8)
    s_iota = sublane_iota(LANES).astype(jnp.int8)
    w_iota = (sublane_iota(2 * LANES) - LANES).astype(jnp.int8)
    left, right = [], []
    for j in range(group):
        here = pl.ds(first + j, 1)
        hit = same(s_iota, s_ref[here, :])
        left.append(jnp.concatenate([jnp.where(hit, spread8(x[here, :], LANES), nil) for x in refs], axis=0))
        right.append(jnp.where(same(w_iota, w_ref[here, :]), one, nil))
    return dot_nt(jnp.concatenate(left, axis=1), jnp.concatenate(right, axis=1))


STEPS = 4


def before(lanes):
    return narrow(sublane_iota(LANES, lanes) < lax.broadcasted_iota(jnp.int32, (LANES, lanes), 1))


def density_kernel(parts, bin_hbm, area_hbm, box_hbm, owner_hbm, dens_ref, top_ref, bottom_ref, starts_ref, s_ref, w_ref, code_ref,
                   a_ref, b_ref, bin_ref, area_ref, box_ref, owner_ref, pre_ref, cnt_ref, raw_ref, cong_ref, sem):
    pairs = ((bin_hbm, bin_ref), (area_hbm, area_ref), (box_hbm, box_ref), (owner_hbm, owner_ref))
    copies = [pltpu.make_async_copy(x, y, sem.at[k]) for k, (x, y) in enumerate(pairs)]
    for copy in copies:
        copy.start()
    raw_ref[...] = jnp.zeros_like(raw_ref)
    cong_ref[...] = jnp.zeros_like(cong_ref)
    copies[0].wait()
    copies[1].wait()
    all_rows = bin_ref.shape[0]
    bins = bin_ref[...]
    area = area_ref[...].astype(F32)
    s_ref[...] = ((bins >> 8) & 1) * TILE_R + (bins >> 9)
    w_ref[...] = (bins & 255) - LANES
    a_ref[...], b_ref[...] = halves(area)
    code_ref[...] = area_code(area) * (TILE_R * TILE_C) + bins
    copies[2].wait()
    copies[3].wait()
    nil = jnp.zeros((), BF16)
    one = jnp.ones((), BF16)
    steps = STEPS
    group = all_rows // steps
    width = box_ref.shape[1] // steps
    r_iota = narrow(sublane_iota(TILE_R, width))
    c_iota = narrow(sublane_iota(TILE_C, width) - TILE_C // 2)
    upper = before(2 * LANES).astype(F8)
    nil8 = jnp.zeros((), F8)
    one8 = jnp.ones((), F8)
    lane = lax.broadcasted_iota(jnp.int32, (group, LANES), 1)
    many = 8

    def step(k, carry):
        raw_ref[...] += placed((a_ref, b_ref), s_ref, w_ref, k * group, group)
        box = box_ref[:, pl.ds(pl.multiple_of(k * width, width), width)].astype(F32)
        tall = box[1:2] - box[0:1] + 1.0
        wide = box[3:4] - box[2:3] + 1.0
        weight = ((tall + wide) / (tall * wide)).astype(BF16).astype(F32)
        big, small = halves(weight)
        rows = (r_iota >= spread(box[0:1], TILE_R)) & (r_iota <= spread(box[1:2], TILE_R))
        middle = float(TILE_C // 2)
        cols = (c_iota >= spread(box[2:3] - middle, TILE_C)) & (c_iota <= spread(box[3:4] - middle, TILE_C))
        cong_ref[...] += dot_nt(
            jnp.where(cols, one, nil).astype(F8),
            jnp.concatenate(
                [jnp.where(rows, spread(x, TILE_R), nil).astype(F8) for x in (big, small * SMALL)], axis=0
            ),
        )
        here = pl.ds(pl.multiple_of(k * group, group), group)
        owner = owner_ref[here, :]
        owner8 = owner.astype(jnp.int8)
        prefix = jnp.zeros((group, LANES), F32)
        counts = jnp.zeros((group, LANES), F32)
        for g in range(0, parts, many):
            hits = [owner == g + m for m in range(many)]
            masks = [jnp.where(owner8 == jnp.int8(g + m), one8, nil8) for m in range(many)]
            sums = jnp.dot(jnp.concatenate(masks, axis=0), upper, preferred_element_type=F32)
            for m in range(many):
                part = sums[m * group : (m + 1) * group]
                prefix = jnp.where(hits[m], part[:, :LANES], prefix)
                counts = jnp.where(lane == g + m, part[:, LANES:], counts)
        pre_ref[here, :] = prefix
        cnt_ref[here, :] = counts
        return carry

    lax.fori_loop(0, steps, step, 0)
    raw = raw_ref[:LANES] + raw_ref[LANES:]
    raw = jnp.concatenate([raw[:TILE_R], raw[TILE_R:]], axis=1)
    cong = cong_ref[...].T
    cong = cong[:TILE_R] + cong[TILE_R:] * (1.0 / SMALL)
    dens = raw * (1.0 + GAMMA * cong)
    dens_ref[...] = dens
    top_ref[...] = dens[:EDGE]
    bottom_ref[...] = dens[TILE_R - EDGE :]

    counts = cnt_ref[...]
    lower = narrow(
        lax.broadcasted_iota(jnp.int32, (all_rows, all_rows), 1)
        < lax.broadcasted_iota(jnp.int32, (all_rows, all_rows), 0)
    )
    base = jnp.dot(lower, counts.astype(BF16), preferred_element_type=F32)
    total = base[all_rows - 8 :] + counts[all_rows - 8 :]
    high = jnp.floor(total * (1.0 / 64.0))
    low = total - high * 64.0
    strict = before(LANES)
    first = jnp.dot(low.astype(BF16), strict, preferred_element_type=F32) + 64.0 * jnp.dot(
        high.astype(BF16), strict, preferred_element_type=F32
    )
    starts = jnp.broadcast_to(first[7:8], (8, LANES))
    starts_ref[...] = starts.astype(jnp.int32)
    dest = (pre_ref[...] + jnp.take_along_axis(base + starts[:1], owner_ref[...], axis=1)).astype(jnp.int32)
    half = all_rows // 2
    top = jnp.where(dest >= half * LANES, 1, 0)
    s_ref[...] = (dest >> 7) - top * half
    w_ref[...] = (dest & (LANES - 1)) + top * LANES - LANES


def order_kernel(parts, starts_ref, s_ref, w_ref, code_ref, slots_ref, sorted_ref, a_ref, b_ref, c_ref, acc_ref, run_bin_ref, run_area_ref):
    all_rows = s_ref.shape[0]
    half = all_rows // 2
    group = all_rows // STEPS
    acc_ref[...] = jnp.zeros_like(acc_ref)

    def encode(k):
        here = pl.ds(pl.multiple_of(k * group, group), group)
        rest, last = divide(code_ref[here, :], BASE)
        first, middle = divide(rest, BASE)
        a_ref[here, :] = symbol(first)
        b_ref[here, :] = symbol(middle)
        c_ref[here, :] = symbol(last)

    def place(k, carry):
        acc_ref[...] += placed((a_ref, b_ref, c_ref), s_ref, w_ref, k * group, group)
        encode(lax.rem(k + 1, STEPS))
        return carry

    encode(0)

    lax.fori_loop(0, STEPS, place, 0)
    for h in range(2):
        out = slice(h * half, (h + 1) * half)
        digits = [
            digit_of(acc_ref[k * half : (k + 1) * half, h * LANES : (h + 1) * LANES]) for k in range(3)
        ]
        code = (digits[0] * BASE + digits[1]) * BASE + digits[2]
        bins = code & (TILE_R * TILE_C - 1)
        sorted_ref[out, :] = bins
        run_bin_ref[out, :] = bins.astype(F32)
        run_area_ref[out, :] = area_of(code >> 15)
    pad = slice(all_rows, run_bin_ref.shape[0])
    run_bin_ref[pad, :] = jnp.zeros((run_bin_ref.shape[0] - all_rows, LANES), F32)
    run_area_ref[pad, :] = jnp.zeros((run_bin_ref.shape[0] - all_rows, LANES), F32)
    expand(parts, starts_ref, all_rows * LANES, ((run_bin_ref, 0, slots_ref, -1.0), (run_area_ref, 1, slots_ref, 0.0)))


def flow_kernel(parts, grid_rows, grid_cols, starts_ref, dens_in, up_ref, down_ref, left_ref, right_ref, sorted_ref,
                dens_ref, slots_ref, pad_ref, hi_ref, lo_ref, row_ref, col_ref, table_ref):
    rows = sorted_ref.shape[0]
    mid = pl.ds(EDGE, TILE_R)
    inner = pl.ds(LANES, TILE_C)
    pad_ref[mid, inner] = dens_in[...]
    pad_ref[:EDGE, inner] = up_ref[...]
    pad_ref[TILE_R + EDGE :, inner] = down_ref[...]
    pad_ref[:, :LANES] = left_ref[...]
    pad_ref[:, LANES + TILE_C :] = right_ref[...]
    tall, wide = pad_ref.shape
    grow = lax.axis_index("rows") * TILE_R + lax.broadcasted_iota(jnp.int32, (tall, 1), 0) - EDGE
    gcol = lax.axis_index("cols") * TILE_C + lax.broadcasted_iota(jnp.int32, (1, wide), 1) - LANES
    open_lower = grow + 1 != grid_rows
    open_upper = grow != 0
    open_right = gcol + 1 != grid_cols
    open_left = gcol != 0
    flow_row = jnp.zeros((TILE_R, TILE_C), F32)
    flow_col = jnp.zeros((TILE_R, TILE_C), F32)
    for step in range(DIFF_STEPS):
        d = pad_ref[...]
        lower = jnp.where(open_lower, pltpu.roll(d, tall - 1, 0) - d, 0.0)
        upper = jnp.where(open_upper, pltpu.roll(d, 1, 0) - d, 0.0)
        right = jnp.where(open_right, pltpu.roll(d, wide - 1, 1) - d, 0.0)
        left = jnp.where(open_left, pltpu.roll(d, 1, 1) - d, 0.0)
        pad_ref[...] = d + RATE * ((lower + upper) + (right + left))
        centre = (slice(EDGE, EDGE + TILE_R), slice(LANES, LANES + TILE_C))
        rate = -0.5 / (d[centre] + 1.0)
        flow_row += (lower - upper)[centre] * rate
        flow_col += (right - left)[centre] * rate
    dens_ref[...] = pad_ref[mid, inner]
    coarse, fine = [], []
    for flow in (flow_row, flow_col):
        table = jnp.concatenate([flow[:, k * LANES : (k + 1) * LANES] for k in range(TILE_C // LANES)], axis=0).T
        big = table.astype(BF16)
        coarse.append(big)
        fine.append((table - big.astype(F32)).astype(BF16))
    table = jnp.concatenate(coarse + fine, axis=0)
    bins = sorted_ref[...]
    hi_ref[:rows] = (((bins >> 7) & 3) * TILE_R + (bins >> 9)).astype(F32)
    lo_ref[:rows] = (bins & (LANES - 1)).astype(F32)
    hi_ref[rows:] = jnp.zeros((hi_ref.shape[0] - rows, LANES), F32)
    lo_ref[rows:] = jnp.zeros((hi_ref.shape[0] - rows, LANES), F32)
    hi_iota = narrow(sublane_iota(256))
    lo_iota = sublane_iota(LANES).astype(F32)
    nil = jnp.zeros((), BF16)
    one = jnp.ones((), BF16)
    for k in range(TILE_C // LANES):
        cols = slice(k * LANES, (k + 1) * LANES)
        out = slice(k * TILE_R, (k + 1) * TILE_R)
        table_ref[0, out, :] = flow_row[:, cols]
        table_ref[1, out, :] = flow_col[:, cols]

    def look_up(step, carry):
        first = step * (DIRECT + BY_DOT)
        here = pl.ds(first, DIRECT)
        row_here, lane_here = hi_ref[here, :], lo_ref[here, :].astype(jnp.int32)
        got = [jnp.zeros((DIRECT, LANES), F32)] * 2
        for k in range(table_ref.shape[1]):
            hit = row_here == float(k)
            for c in range(2):
                line = jnp.broadcast_to(table_ref[c, k : k + 1, :], (DIRECT, LANES))
                near = jnp.take_along_axis(line, lane_here, axis=1, mode="promise_in_bounds")
                got[c] = jnp.where(hit, near, got[c])
        row_ref[here, :] = got[0]
        col_ref[here, :] = got[1]
        picks = jnp.concatenate(
            [
                jnp.where(hi_iota == spread(hi_ref[pl.ds(first + DIRECT + k, 1), :], 256), one, nil)
                for k in range(BY_DOT)
            ],
            axis=1,
        )
        found = jnp.dot(table, picks, preferred_element_type=F32)
        for k in range(BY_DOT):
            here = pl.ds(first + DIRECT + k, 1)
            hit = lo_iota == lo_ref[here, :]
            part = found[:, k * LANES : (k + 1) * LANES]
            both = part[: 2 * LANES] + part[2 * LANES :]
            row_ref[here, :] = jnp.sum(jnp.where(hit, both[:LANES], 0.0), axis=0, keepdims=True)
            col_ref[here, :] = jnp.sum(jnp.where(hit, both[LANES:], 0.0), axis=0, keepdims=True)
        return carry

    lax.fori_loop(0, -(-rows // (DIRECT + BY_DOT)), look_up, 0)
    pad = slice(rows, row_ref.shape[0])
    row_ref[pad, :] = jnp.zeros((row_ref.shape[0] - rows, LANES), F32)
    col_ref[pad, :] = jnp.zeros((row_ref.shape[0] - rows, LANES), F32)
    expand(parts, starts_ref, rows * LANES, ((row_ref, 0, slots_ref, 0.0), (col_ref, 1, slots_ref, 0.0)))


def merge_kernel(first_ref, second_ref, out_ref, bin_ref):
    parts, _, per, _ = first_ref.shape

    def one_source(k, carry):
        bin_ref[pl.ds(pl.multiple_of(k * per, per), per), :] = first_ref[k, 0].astype(jnp.int32)
        for r in range(per):
            row = slice(r, r + 1)
            cells = jnp.concatenate([second_ref[k, 0, row, :], second_ref[k, 1, row, :], first_ref[k, 1, row, :]], axis=0)
            out_ref[:, pl.ds(pl.multiple_of((k * per + r) * LANES, LANES), LANES)] = cells
        return carry

    lax.fori_loop(0, parts, one_source, 0, unroll=4)


def shape(*dims, dtype=F32):
    return jax.ShapeDtypeStruct(dims, dtype)


def vmem(*dims, dtype=F32):
    return pltpu.VMEM(dims, dtype)


def on_device(cell_bin, cell_area, owner, net_box):
    parts = lax.axis_size(("rows", "cols"))
    count = cell_bin.shape[0]
    rows = count // LANES
    capacity = 2 * count // parts
    per = capacity // LANES
    spare = -(-max(per + 1, -rows % (DIRECT + BY_DOT)) // 8) * 8
    bins = cell_bin.reshape(rows, LANES)
    area = cell_area.reshape(rows, LANES)
    n_rows, n_cols = lax.axis_size("rows"), lax.axis_size("cols")
    grid_rows, grid_cols = n_rows * TILE_R, n_cols * TILE_C
    owner = owner.reshape(rows, LANES)
    cells = vmem(rows, LANES)
    runs = vmem(rows + spare, LANES)
    table = shape(rows, LANES)
    grant = pltpu.CompilerParams(vmem_limit_bytes=GRANT)
    int_cells = vmem(rows, LANES, dtype=jnp.int32)
    dens, top, bottom, starts, s, w, codes = pl.pallas_call(
        functools.partial(density_kernel, parts),
        out_shape=(vmem(TILE_R, TILE_C), vmem(EDGE, TILE_C), vmem(EDGE, TILE_C), shape(8, LANES, dtype=jnp.int32),
                   int_cells, int_cells, int_cells),
        in_specs=[pl.BlockSpec(memory_space=pltpu.HBM)] * 4,
        scratch_shapes=[cells, cells, int_cells, vmem(rows, LANES, dtype=BF16), vmem(*net_box.shape, dtype=jnp.int32), int_cells, cells, cells,
                        vmem(2 * LANES, 2 * LANES), vmem(TILE_C, 2 * TILE_R), pltpu.SemaphoreType.DMA((4,))],
        compiler_params=pltpu.CompilerParams(vmem_limit_bytes=FULL),
        name="density",
    )(bins, area, net_box, owner)
    ahead = [(k, k + 1) for k in range(n_rows - 1)]
    behind = [(k + 1, k) for k in range(n_rows - 1)]
    up = lax.ppermute(bottom, "rows", ahead)
    down = lax.ppermute(top, "rows", behind)
    scalars = pl.BlockSpec(memory_space=pltpu.SMEM)
    slots, in_order = pl.pallas_call(
        functools.partial(order_kernel, parts),
        out_shape=(vmem(parts, 2, per, LANES), int_cells),
        in_specs=[scalars] + [pl.BlockSpec()] * 3,
        scratch_shapes=[cells, cells, cells, vmem(3 * LANES, 2 * LANES), runs, runs],
        compiler_params=grant,
        cost_estimate=pl.CostEstimate(flops=15_000_000_000, bytes_accessed=2_000_000, transcendentals=0),
        name="order",
    )(starts, s, w, codes)
    up, down, slots = lax.optimization_barrier((up, down, slots))
    strip = jnp.concatenate([up, dens, down], axis=0)
    ahead = [(k, k + 1) for k in range(n_cols - 1)]
    behind = [(k + 1, k) for k in range(n_cols - 1)]
    left = lax.ppermute(strip[:, TILE_C - LANES :], "cols", ahead)
    right = lax.ppermute(strip[:, :LANES], "cols", behind)
    first = lax.all_to_all(slots, ("rows", "cols"), 0, 0, tiled=True)
    density, shifts = pl.pallas_call(
        functools.partial(flow_kernel, parts, grid_rows, grid_cols),
        out_shape=(shape(TILE_R, TILE_C), vmem(parts, 2, per, LANES)),
        in_specs=[scalars] + [pl.BlockSpec()] * 6,
        scratch_shapes=[vmem(TILE_R + 2 * EDGE, TILE_C + 2 * LANES), *[vmem(rows + spare, LANES)] * 4, vmem(2, 256, LANES)],
        compiler_params=grant,
        cost_estimate=pl.CostEstimate(flops=15_000_000_000, bytes_accessed=2_000_000, transcendentals=0),
        name="flow",
    )(starts, dens, up, down, left, right, in_order)
    second = lax.all_to_all(shifts, ("rows", "cols"), 0, 0, tiled=True)
    if per % 8:
        migrated = jnp.stack([second[:, 0].reshape(-1), second[:, 1].reshape(-1), first[:, 1].reshape(-1)])
        return density, migrated, first[:, 0].reshape(-1).astype(jnp.int32)
    migrated, migrated_bin = pl.pallas_call(
        merge_kernel,
        out_shape=(shape(3, parts * capacity), shape(parts * per, LANES, dtype=jnp.int32)),
        compiler_params=grant,
        name="merge",
    )(first, second)
    return density, migrated, migrated_bin.reshape(-1)


def solution(mesh):
    both = ("rows", "cols")
    in_specs = (P(both), P(both), P(both), P(None, both))
    out_specs = (P("rows", "cols"), P(None, both), P(both))
    return jax.shard_map(on_device, mesh=mesh, in_specs=in_specs, out_specs=out_specs, check_vma=False)
```
